32 devices in a mesh: row: 4 (over x, core), col: 8 (over z, y).
Axes of the slice: x: 2, y: 2, z: 4, core: 2. Of those that a mesh axis runs over, the one named last changes fastest.
Arguments:
- rhs: float32 [32768, 512], P('col', 'row'), may hold values from -6 to 6
- factors: bfloat16 [32768, 2048], P('col', 'row'), may hold values from -0.15625 to 0.15625
- diag_inv: float32 [4, 512, 512], replicated, may hold values from -2 to 2, as said below
Outputs:
- solution: float32 [32768, 512], P('col', 'row')
The draws below stay inside these ranges and needn't reach their ends.
Inputs may be any that keep to these rules, and one draw needn't show every extreme that they name: `diag_inv`: entries off the diagonal of each block lie within 2 / sqrt(512) in magnitude; diagonal entries lie in 0.5 to 2.
All inputs are finite; a program needn't handle non-finite values.
Results may differ from the reference program's by a relative error of at most 0.0038.
Values may be sent and summed in bfloat16 or wider, within the bound.
A program may use at most 128 MiB of HBM per device.

```python
import jax
import jax.numpy as jnp
from jax import lax

NB = 512
STEPS = 4
NW = 2048
ROWS = 32768
SPAN = 8192
RHS = 512


def draw_diag_inv(key, part):
    base = jax.random.fold_in(key, 7)
    key_low, key_up, key_dia = jax.random.split(base, 3)
    scale = 0.5 / jnp.sqrt(jnp.float32(NB))
    lower_part = jnp.clip(jax.random.normal(key_low, (STEPS, NB, NB), jnp.float32), -4.0, 4.0) * scale
    upper_part = jnp.clip(jax.random.normal(key_up, (STEPS, NB, NB), jnp.float32), -4.0, 4.0) * scale
    diagonal = jnp.exp(jax.random.uniform(key_dia, (STEPS, NB), jnp.float32, jnp.log(0.5), jnp.log(2.0)))
    index = jnp.arange(NB)
    below = index[:, None] > index[None, :]
    above = index[:, None] < index[None, :]
    packed = jnp.where(below[None], lower_part, jnp.where(above[None], upper_part, 0.0))
    return (packed + diagonal[:, :, None] * jnp.eye(NB, dtype=jnp.float32)[None]).astype(jnp.float32)


def block_levels(own_key, shape, cuts, smallest, high):
    loudness = 1.0
    for dim, blocks in cuts:
        draws = jax.random.uniform(jax.random.fold_in(jax.random.fold_in(own_key, 6), dim), (blocks,), jnp.float32, smallest / len(cuts), high / len(cuts))
        loudness = loudness * jnp.repeat(jnp.exp(draws), shape[dim] // blocks).reshape((-1,) + (1,) * (len(shape) - 1 - dim))
    return loudness


def gaussian(rng, extent, scale, most, shards=(), held_as=jnp.bfloat16):
    factor_of = block_levels(rng, extent, shards, -0.22, 0.18) if shards else 1.0
    values = jax.random.normal(rng, extent, jnp.float32) * scale * factor_of
    return jnp.minimum(jnp.maximum(values, -most), most).astype(held_as)


def setup_inputs(seed: int = 0) -> dict:
    arg_keys = jax.random.split(jax.random.key(seed), 4)
    rhs = gaussian(arg_keys[0], (ROWS, RHS), 1.0, 6.0, ((0, 8), (1, 4)), jnp.float32)
    factors = gaussian(arg_keys[1], (ROWS, NW), (16 * NW // 25) ** -0.5, 0.15625, ((0, 8), (1, 4)))
    diag_inv = draw_diag_inv(jax.random.fold_in(arg_keys[3], 71), 0)
    return dict(rhs=rhs, factors=factors, diag_inv=diag_inv)


def reference(rhs, factors, diag_inv):
    index = jnp.arange(NB)
    strict_lower = index[:, None] > index[None, :]
    eye = jnp.eye(NB, dtype=jnp.float32)
    work = rhs.astype(jnp.float32)
    for step in range(STEPS):
        lower_inv = jnp.where(strict_lower, diag_inv[step], jnp.float32(0.0)) + eye
        first = step * SPAN
        solved = jnp.dot(lower_inv, work[first:first + NB], precision=lax.Precision.HIGHEST, preferred_element_type=jnp.float32)
        work = work.at[first:first + NB].set(solved)
        below = first + NB
        if below < ROWS:
            product = jnp.dot(factors[below:, step * NB:(step + 1) * NB], solved.astype(jnp.bfloat16), preferred_element_type=jnp.float32)
            work = work.at[below:].add(-product)
    for step in reversed(range(STEPS)):
        upper_inv = jnp.triu(diag_inv[step])
        first = step * SPAN
        solved = jnp.dot(upper_inv, work[first:first + NB], precision=lax.Precision.HIGHEST, preferred_element_type=jnp.float32)
        work = work.at[first:first + NB].set(solved)
        if first > 0:
            product = jnp.dot(factors[:first, step * NB:(step + 1) * NB], solved.astype(jnp.bfloat16), preferred_element_type=jnp.float32)
            work = work.at[:first].add(-product)
    return work
```

```python
import functools

import jax
import jax.numpy as jnp
from jax import lax
from jax.experimental import pallas as pl
from jax.experimental.pallas import tpu as pltpu
from jax.sharding import PartitionSpec as P

MESH = pl.DeviceIdType.MESH
F32 = jnp.float32
BF16 = jnp.bfloat16
CHUNKS = 8
SUBS = 2
CUTS = 2
GATHER = 3


def remote(src, dst, send_sem, recv_sem, **device):
    return pltpu.make_async_remote_copy(
        src_ref=src,
        dst_ref=dst,
        send_sem=send_sem,
        recv_sem=recv_sem,
        device_id=device,
        device_id_type=MESH,
    )


def dot(a, b):
    return jnp.dot(a, b, preferred_element_type=F32)


def dot_t(a, b):
    return lax.dot_general(a, b, (((1,), (1,)), ((), ())), preferred_element_type=F32)


def split(value):
    high = value.astype(BF16)
    return high, (value - high.astype(F32)).astype(BF16)


def kernel(
    n_row, n_col, steps, block,
    rhs_hbm, factors_hbm, diag_ref, out_ref,
    rhs_ref, factors_ref, extra,
    diag, low_hi, low_lo, up_hi, up_lo, panel, solved, last, work, state, gathered,
    send1, recv1, own1, send2, recv2,
    diag_sem, f_send, f_far, f_recv, f_fwd, s_chain, s_side, s_row, s_recv, s_last, g_local, g_recv,
    one_send, one_recv, two_send, two_recv, x_send, x_recv, x_fwd, load_sem,
):
    rows_dev, width = rhs_hbm.shape
    cols = factors_ref.shape[1]
    pieces = block // cols
    chips = n_row // 2
    side = n_col // steps
    row = lax.axis_index("row")
    col = lax.axis_index("col")
    chip, core = row // 2, row % 2
    sibling = chip * 2 + 1 - core
    zone, lane = col // side, col % side
    owner = lane == 0
    base = zone * side

    diag_copy = pltpu.make_async_copy(diag_ref.at[zone], diag, diag_sem)
    rhs_copy = pltpu.make_async_copy(rhs_hbm.at[pl.ds(0, block)], rhs_ref, load_sem.at[0])
    factors_copy = pltpu.make_async_copy(factors_hbm, factors_ref, load_sem.at[1])
    work_copy = pltpu.make_async_copy(rhs_hbm.at[pl.ds(0, block)], work, load_sem.at[2])
    panel_own = pltpu.make_async_copy(factors_hbm.at[pl.ds(0, block)], panel.at[row], load_sem.at[3])
    diag_copy.start()
    work_copy.start()
    panel_own.start()
    factors_copy.start()
    rhs_copy.start()

    barrier = pltpu.get_barrier_semaphore()
    for d in range(1, n_row):
        pl.semaphore_signal(barrier, inc=1, device_id={"row": (row + d) % n_row}, device_id_type=MESH)

    def greet(other):
        pl.semaphore_signal(barrier, inc=1, device_id={"col": other}, device_id_type=MESH)

    @pl.when(owner)
    def _():
        for d in range(1, side):
            greet(base + d)

    pl.when(jnp.logical_and(owner, zone > 0))(lambda: greet(base - side))
    pl.when(jnp.logical_and(owner, zone < steps - 1))(lambda: greet(base + side))
    pl.when(jnp.logical_not(owner))(lambda: greet(base))
    ends = jnp.where(zone > 0, 1, 0) + jnp.where(zone < steps - 1, 1, 0)
    pl.semaphore_wait(barrier, n_row - 1 + jnp.where(owner, ends + side - 1, 1))

    far = [((chip + d) % chips) * 2 + core for d in range(1, chips)]
    sends_panel = jnp.logical_and(owner, row // pieces != zone)
    half = block // 2
    cut_rows = half // CUTS
    pair = chip * 2
    later = pair // pieces > zone
    leading = jnp.where(later, pair + 1, pair)
    trailing = jnp.where(later, pair, pair + 1)

    def cut(h, c):
        return pl.ds(pl.multiple_of(h * half + c * cut_rows, cut_rows), cut_rows)

    def needed(source):
        return jnp.logical_and(owner, source // pieces != zone)

    def near_copy(h, c):
        rows = cut(h, c)
        return remote(factors_hbm.at[rows], panel.at[row, rows], f_send.at[h, c], f_recv.at[row, h, c], row=sibling)

    def far_copy(source, d, c):
        piece = panel.at[source, cut(core, c)]
        return remote(piece, piece, f_far.at[source % 2, d - 1, c], f_recv.at[source, core, c], row=far[d - 1])

    def relay_copy(source, h, c):
        piece = panel.at[source, cut(h, c)]
        return remote(piece, piece, f_fwd.at[source, c], f_recv.at[source, h, c], row=sibling)

    @pl.when(sends_panel)
    def _():
        for h in (1 - core, core):
            for c in range(CUTS):
                near_copy(h, c).start()

    def far_sends(source):
        @pl.when(needed(source))
        def _():
            @pl.when(source != row)
            def _():
                for c in range(CUTS):
                    relay_copy(source, core, c).wait_recv()

            for d in range(1, chips):
                for c in range(CUTS):
                    far_copy(source, d, c).start()

    panel_own.wait()
    pl.when(leading == row)(lambda: far_sends(leading))

    step_rows = rows_dev // CHUNKS
    n_extra = jnp.maximum(GATHER - (zone + 1) // 2 - jnp.where(owner, 1, 0), 0)

    def span(m):
        return pl.ds(pl.multiple_of(m * step_rows, step_rows), step_rows)

    def extra_copy(g, d):
        return remote(
            factors_hbm.at[span(CHUNKS - 1 - g)], extra.at[g, row], x_send.at[g, d], x_recv.at[g, row],
            row=far[d - 1] if d else sibling,
        )

    def extra_forward(g, source):
        return remote(extra.at[g, source], extra.at[g, source], x_fwd.at[g, source // 2], x_recv.at[g, source], row=sibling)

    def extra_start(g, carry):
        for d in range(chips):
            extra_copy(g, d).start()
        return carry

    waits = jnp.logical_and(owner, zone > 0)
    lax.fori_loop(0, jnp.where(owner, 0, n_extra), extra_start, 0)
    diag_copy.wait()
    work_copy.wait()

    @pl.when(owner)
    def _():
        down = lax.broadcasted_iota(jnp.int32, (block, block), 0)
        across = lax.broadcasted_iota(jnp.int32, (block, block), 1)
        matrix = diag[...]
        low_hi[...], low_lo[...] = split(jnp.where(down > across, matrix, 0.0))
        up_hi[...], up_lo[...] = split(jnp.where(down <= across, matrix, 0.0))
        state[...] = work[...].T

    sub = width // SUBS

    def batch(s, start=0):
        return pl.ds(pl.multiple_of(start + s * sub, sub), sub)

    def stacked(value):
        high, low = split(value)
        return high, jnp.concatenate([high, low])

    def folded(both, more):
        return both[:sub] + (both[sub:] + more)

    def solve_low(value):
        high, both = stacked(value)
        top = folded(dot_t(both[:, :half], low_hi[:half, :half]), dot_t(high[:, :half], low_lo[:half, :half]))
        return jnp.concatenate([top, folded(dot_t(both, low_hi[half:]), dot_t(high, low_lo[half:]))], axis=1)

    def solve_up(value):
        high, both = stacked(value)
        end = folded(dot_t(both[:, half:], up_hi[half:, half:]), dot_t(high[:, half:], up_lo[half:, half:]))
        return jnp.concatenate([folded(dot_t(both, up_hi[:half]), dot_t(high, up_lo[:half])), end], axis=1)

    def slot(t):
        return jnp.where(t <= zone, t, steps + zone - t)

    def is_far(source):
        return jnp.logical_and(owner, source // 2 != chip)

    def relay_panel(j):
        for p in range(pieces):
            source = j * pieces + p

            @pl.when(is_far(source))
            def _():
                for c in range(CUTS):
                    relay_copy(source, core, c).wait_recv()
                    relay_copy(source, core, c).start()

    def relay_back():
        def one(i, carry):
            relay_panel(steps - 1 - i)
            return carry

        lax.fori_loop(0, steps - 1 - zone, one, 0)

    def arrive_panel(j):
        for p in range(pieces):
            source = j * pieces + p

            @pl.when(source != row)
            def _():
                for c in range(CUTS):
                    relay_copy(source, 1 - core, c).wait_recv()

    def chain_copy(t, j, s):
        target = jnp.where(t <= zone, zone + 1, zone - 1)
        piece = solved.at[j, batch(s)]
        return remote(piece, piece, s_chain.at[t, s], s_recv.at[j, s], col=target * side)

    def chain_sends(t):
        return jnp.where(t <= zone, zone < steps - 1, zone > 0)

    def side_copy(t, j, d, s):
        piece = solved.at[j, batch(s)]
        return remote(piece, piece, s_side.at[t, d, s], s_recv.at[j, s], col=base + d)

    def row_copy(t, j, s, p):
        return remote(
            solved.at[j, batch(s), pl.ds(p * cols, cols)], gathered.at[core, batch(s, chip * width)],
            s_row.at[t, s, p], g_recv.at[row, s], row=j * pieces + p,
        )

    def local_copy(j, s, p):
        return pltpu.make_async_copy(
            solved.at[j, batch(s), pl.ds(p * cols, cols)], gathered.at[core, batch(s, chip * width)], g_local.at[s]
        )

    def pass_on(t, j, s):
        pl.when(jnp.logical_and(owner, chain_sends(t)))(lambda: chain_copy(t, j, s).start())

        @pl.when(owner)
        def _():
            for d in range(1, side):
                side_copy(t, j, d, s).start()

        for p in range(pieces):
            pl.when(j * pieces + p != row)(lambda: row_copy(t, j, s, p).start())
            pl.when(j * pieces + p == row)(lambda: local_copy(j, s, p).start())

    def update(j, s):
        total = state[batch(s)]
        for p in range(pieces):
            total = total - dot_t(solved[j, batch(s), pl.ds(p * cols, cols)], panel[j * pieces + p])
        state[batch(s)] = total

    def solve_first(s):
        value = state[batch(s)]
        value = value + solve_low(value)
        state[batch(s)] = value
        solved[zone, batch(s)] = value.astype(BF16)
        pass_on(zone, zone, s)

    def last_copy(s):
        target = jnp.where(zone > 0, zone - 1, 0) * side
        return remote(last.at[batch(s)], solved.at[zone, batch(s)], s_last.at[s], s_recv.at[zone, s], col=target)

    def solve_last(s):
        value = solve_up(state[batch(s)])
        state[batch(s)] = value
        last[batch(s)] = value.astype(BF16)
        pl.when(zone > 0)(lambda: last_copy(s).start())

    def one_copy(m):
        return remote(send1.at[m], recv1.at[m], one_send.at[m], one_recv.at[m], row=sibling)

    def two_copy(m, d):
        return remote(send2.at[m, d - 1], recv2.at[m, d - 1], two_send.at[m, d - 1], two_recv.at[m, d - 1], row=far[d - 1])

    def first(m, carry):
        send1[m] = dot_t(factors_ref[span(m)], gathered[1 - core]).astype(BF16)
        one_copy(m).start()
        return carry

    def second(m, carry):
        @pl.when(m + 1 < n_swap)
        def _():
            first(m + 1, 0)

        own1[m] = dot_t(factors_ref[span(m)], gathered[core])
        one_copy(m).wait_recv()
        for d in range(1, chips):
            there = pl.ds(pl.multiple_of(((chip + d) % chips) * width, width), width)
            send2[m, d - 1] = (own1[m, :, there] + recv1[m, :, there].astype(F32)).astype(BF16)
            two_copy(m, d).start()
        return carry

    def third(m, carry):
        here = pl.ds(pl.multiple_of(chip * width, width), width)
        total = own1[m, :, here] + recv1[m, :, here].astype(F32)
        for d in range(1, chips):
            two_copy(m, d).wait_recv()
            total = total + recv2[m, d - 1].astype(F32)
        out_ref[span(m)] = total
        return carry

    def finish(m, carry):
        one_copy(m).wait_send()
        for d in range(1, chips):
            two_copy(m, d).wait_send()
        return carry

    n_swap = CHUNKS - n_extra

    def extra_hand_on(g, carry):
        for d in range(1, chips):
            extra_forward(g, far[d - 1]).wait_recv()
            extra_forward(g, far[d - 1]).start()
        return carry

    def extra_product(g, carry):
        rows = span(CHUNKS - 1 - g)
        total = jnp.zeros((step_rows, width), F32)
        for d in range(n_row):
            source = (row + d) % n_row
            part_of = solved[source // pieces, :, pl.ds(pl.multiple_of((source % pieces) * cols, cols), cols)]
            if d == 0:
                total = total + dot_t(factors_ref[rows], part_of)
            else:
                @pl.when(source % 2 != core)
                def _():
                    extra_forward(g, source).wait_recv()

                total = total + dot_t(extra[g, source], part_of)
        out_ref[rows] = total
        return carry

    def extra_finish(g, carry):
        for d in range(chips):
            extra_copy(g, d).wait_send()
        for d in range(1, chips):
            extra_forward(g, far[d - 1]).wait_send()
        return carry

    def first_products():
        factors_copy.wait()
        rhs_copy.wait()

        def arrive(s, carry):
            local_copy(0, s, 0).wait()
            for d in range(1, n_row):
                source = (row + d) % n_row
                piece = gathered.at[source % 2, batch(s, (source // 2) * width)]
                remote(piece, piece, g_local.at[s], g_recv.at[source, s], row=source).wait_recv()
            return carry

        lax.fori_loop(0, SUBS, arrive, 0)
        first(0, 0)

    def batches(what):
        def one(s, carry):
            what(s)
            return carry

        lax.fori_loop(0, SUBS, one, 0)

    @pl.when(owner)
    def _():
        pl.when(zone == 0)(lambda: batches(solve_first))
        pl.when(leading != row)(lambda: far_sends(leading))
        far_sends(trailing)
        lax.fori_loop(0, jnp.where(zone == 0, n_extra, 0), extra_start, 0)
        pl.when(zone == 0)(relay_back)

        def hop(i, carry):
            t = jnp.where(i < zone, i, i + 1)
            j = slot(t)

            late = jnp.logical_and(is_far(j * pieces), i < zone)

            def take(s):
                chain_copy(t, j, s).wait_recv()
                pass_on(t, j, s)

            @pl.when(late)
            def _():
                batches(take)
                relay_panel(j)

            def one(s):
                pl.when(jnp.logical_not(late))(lambda: take(s))
                pl.when(s == 0)(lambda: arrive_panel(j))
                update(j, s)
                pl.when(i + 1 == zone)(lambda: solve_first(s))
                pl.when(jnp.logical_and(i == steps - 2, zone > 0))(lambda: solve_last(s))

            batches(one)
            lax.fori_loop(0, jnp.where(jnp.logical_and(waits, i == 0), n_extra, 0), extra_start, 0)
            pl.when(i + 1 == zone)(relay_back)
            return carry

        lax.fori_loop(0, steps - 1, hop, 0)

    @pl.when(jnp.logical_not(owner))
    def _():
        def hop(t, carry):
            j = slot(t)

            def one(s):
                chain_copy(t, j, s).wait_recv()
                pass_on(t, j, s)

            batches(one)
            return carry

        lax.fori_loop(0, steps, hop, 0)

    first_products()
    lax.fori_loop(0, n_swap, second, 0)
    lax.fori_loop(0, n_extra, extra_hand_on, 0)
    pl.when(jnp.logical_and(owner, zone == 0))(lambda: batches(solve_last))
    lax.fori_loop(0, n_extra, extra_product, 0)
    lax.fori_loop(0, n_swap, third, 0)

    @pl.when(owner)
    def _():
        out_ref[pl.ds(0, block)] = rhs_ref[...] - state[...].T

    lax.fori_loop(0, n_swap, finish, 0)
    lax.fori_loop(0, n_extra, extra_finish, 0)

    @pl.when(sends_panel)
    def _():
        for h in range(2):
            for c in range(CUTS):
                near_copy(h, c).wait_send()

    for source in (pair, pair + 1):
        @pl.when(needed(source))
        def _():
            for d in range(1, chips):
                for c in range(CUTS):
                    far_copy(source, d, c).wait_send()

    def drain(t, carry):
        j = slot(t)

        for p in range(pieces):
            source = j * pieces + p

            @pl.when(jnp.logical_and(is_far(source), t != zone))
            def _():
                for c in range(CUTS):
                    relay_copy(source, core, c).wait_send()

        def one(s):
            pl.when(jnp.logical_and(owner, chain_sends(t)))(lambda: chain_copy(t, j, s).wait_send())

            @pl.when(owner)
            def _():
                for d in range(1, side):
                    side_copy(t, j, d, s).wait_send()

            for p in range(pieces):
                pl.when(j * pieces + p != row)(lambda: row_copy(t, j, s, p).wait_send())

        batches(one)
        return carry

    lax.fori_loop(0, steps, drain, 0)

    @pl.when(jnp.logical_and(owner, zone > 0))
    def _():
        batches(lambda s: last_copy(s).wait_send())


def body(rhs, factors, diag_inv):
    n_row, n_col = lax.axis_size("row"), lax.axis_size("col")
    rows_dev, width = rhs.shape
    cols = factors.shape[1]
    steps, block = diag_inv.shape[:2]
    pieces, chips, side = block // cols, n_row // 2, n_col // steps
    step_rows = rows_dev // CHUNKS
    dma = pltpu.SemaphoreType.DMA
    vmem = pl.BlockSpec(memory_space=pltpu.VMEM)
    taken = pl.pallas_call(
        functools.partial(kernel, n_row, n_col, steps, block),
        out_shape=jax.ShapeDtypeStruct(rhs.shape, F32),
        in_specs=[pl.BlockSpec(memory_space=pl.ANY)] * 3,
        out_specs=vmem,
        scratch_shapes=[
            pltpu.VMEM((block, width), F32),
            pltpu.VMEM(factors.shape, BF16),
            pltpu.VMEM((GATHER, n_row, step_rows, cols), BF16),
            pltpu.VMEM((block, block), F32),
            pltpu.VMEM((block, block), BF16),
            pltpu.VMEM((block, block), BF16),
            pltpu.VMEM((block, block), BF16),
            pltpu.VMEM((block, block), BF16),
            pltpu.VMEM((n_row, block, cols), BF16),
            pltpu.VMEM((steps, width, block), BF16),
            pltpu.VMEM((width, block), BF16),
            pltpu.VMEM((block, width), F32),
            pltpu.VMEM((width, block), F32),
            pltpu.VMEM((2, chips * width, cols), BF16),
            pltpu.VMEM((CHUNKS, step_rows, chips * width), BF16),
            pltpu.VMEM((CHUNKS, step_rows, chips * width), BF16),
            pltpu.VMEM((CHUNKS, step_rows, chips * width), F32),
            pltpu.VMEM((CHUNKS, chips - 1, step_rows, width), BF16),
            pltpu.VMEM((CHUNKS, chips - 1, step_rows, width), BF16),
            dma, dma((2, CUTS)), dma((2, chips - 1, CUTS)), dma((n_row, 2, CUTS)), dma((n_row, CUTS)),
            dma((steps, SUBS)), dma((steps, side, SUBS)), dma((steps, SUBS, pieces)), dma((steps, SUBS)), dma((SUBS,)),
            dma((SUBS,)), dma((n_row, SUBS)),
            dma((CHUNKS,)), dma((CHUNKS,)), dma((CHUNKS, chips - 1)), dma((CHUNKS, chips - 1)),
            dma((GATHER, chips)), dma((GATHER, n_row)), dma((GATHER, chips)), dma((4,)),
        ],
        compiler_params=pltpu.CompilerParams(
            collective_id=0, has_side_effects=True, vmem_limit_bytes=50 * 1024 * 1024
        ),
    )(rhs, factors, diag_inv)
    return rhs - taken


def solution(mesh):
    placed = (P("col", "row"), P("col", "row"), P())
    return jax.shard_map(
        body, mesh=mesh, in_specs=placed, out_specs=P("col", "row"), check_vma=False
    )
```

```python
import functools

import jax
import jax.numpy as jnp
from jax import lax
from jax.experimental import pallas as pl
from jax.experimental.pallas import tpu as pltpu
from jax.sharding import PartitionSpec as P

MESH = pl.DeviceIdType.MESH
F32 = jnp.float32
BF16 = jnp.bfloat16
CHUNKS = 8
SUBS = 2
CUTS = 2
GATHER = 4
NEAR0, FAR0, NEAR1, FAR1, REST1 = 2, 3, 4, 4, 2
HEAD0, HEAD1 = 2, 4


def remote(src, dst, send_sem, recv_sem, **device):
    return pltpu.make_async_remote_copy(
        src_ref=src,
        dst_ref=dst,
        send_sem=send_sem,
        recv_sem=recv_sem,
        device_id=device,
        device_id_type=MESH,
    )


def dot(a, b):
    return jnp.dot(a, b, preferred_element_type=F32)


def dot_t(a, b):
    return lax.dot_general(a, b, (((1,), (1,)), ((), ())), preferred_element_type=F32)


def split(value):
    high = value.astype(BF16)
    return high, (value - high.astype(F32)).astype(BF16)


def kernel(
    n_row, n_col, steps, block,
    rhs_hbm, factors_hbm, diag_ref, out_ref,
    rhs_ref, factors_ref, extra, taken,
    diag, low_hi, low_lo, up_hi, up_lo, panel, solved, last, work, state, gathered,
    send1, recv1, own1, send2, recv2,
    diag_sem, f_send, f_far, f_recv, f_fwd, s_chain, s_side, s_row, s_lend, s_help, s_hint, s_recv, l_recv, s_last, g_local, g_recv,
    one_send, one_recv, two_send, two_recv, x_send, x_recv, x_fwd, load_sem, out_sem,
):
    rows_dev, width = rhs_hbm.shape
    cols = factors_ref.shape[1]
    pieces = block // cols
    chips = n_row // 2
    side = n_col // steps
    row = lax.axis_index("row")
    col = lax.axis_index("col")
    chip, core = row // 2, row % 2
    sibling = chip * 2 + 1 - core
    zone, lane = col // side, col % side
    owner = lane == 0
    helper = lane == 1
    base = zone * side

    diag_copy = pltpu.make_async_copy(diag_ref.at[zone], diag, diag_sem)
    rhs_copy = pltpu.make_async_copy(rhs_hbm.at[pl.ds(0, block)], rhs_ref, load_sem.at[0])
    factors_copy = pltpu.make_async_copy(factors_hbm, factors_ref, load_sem.at[1])
    work_copy = pltpu.make_async_copy(rhs_hbm.at[pl.ds(0, block)], work, load_sem.at[2])
    panel_own = pltpu.make_async_copy(factors_hbm.at[pl.ds(0, block)], panel.at[row], load_sem.at[3])
    @pl.when(owner)
    def _():
        diag_copy.start()
        work_copy.start()
        panel_own.start()


    barrier = pltpu.get_barrier_semaphore()
    for d in range(1, n_row):
        pl.semaphore_signal(barrier, inc=1, device_id={"row": (row + d) % n_row}, device_id_type=MESH)

    def greet(other):
        pl.semaphore_signal(barrier, inc=1, device_id={"col": other}, device_id_type=MESH)

    @pl.when(owner)
    def _():
        for d in range(1, side):
            greet(base + d)

    pl.when(jnp.logical_and(owner, zone > 0))(lambda: greet(base - side))
    pl.when(jnp.logical_and(owner, zone < steps - 1))(lambda: greet(base + side))
    pl.when(jnp.logical_not(owner))(lambda: greet(base))
    for z in range(1, steps - 2):
        pl.when(jnp.logical_and(owner, zone > z + 1))(lambda: greet(z * side + 1))
    beyond = jnp.where(jnp.logical_and(zone > 0, zone < steps - 2), steps - 2 - zone, 0)
    ends = jnp.where(zone > 0, 1, 0) + jnp.where(zone < steps - 1, 1, 0)

    far = [((chip + d) % chips) * 2 + core for d in range(1, chips)]
    sends_panel = jnp.logical_and(owner, row // pieces != zone)
    half = block // 2
    cut_rows = half // CUTS
    pair = chip * 2
    later = pair // pieces > zone
    leading = jnp.where(later, pair + 1, pair)
    trailing = jnp.where(later, pair, pair + 1)

    def cut(h, c):
        return pl.ds(pl.multiple_of(h * half + c * cut_rows, cut_rows), cut_rows)

    def needed(source):
        return jnp.logical_and(owner, source // pieces != zone)

    def near_copy(h, c):
        rows = cut(h, c)
        return remote(factors_hbm.at[rows], panel.at[row, rows], f_send.at[h, c], f_recv.at[row, h, c], row=sibling)

    def far_copy(source, d, c):
        piece = panel.at[source, cut(core, c)]
        return remote(piece, piece, f_far.at[source % 2, d - 1, c], f_recv.at[source, core, c], row=far[d - 1])

    def relay_copy(source, h, c):
        piece = panel.at[source, cut(h, c)]
        return remote(piece, piece, f_fwd.at[source, c], f_recv.at[source, h, c], row=sibling)

    def far_sends(source):
        @pl.when(needed(source))
        def _():
            @pl.when(source != row)
            def _():
                for c in range(CUTS):
                    relay_copy(source, core, c).wait_recv()

            for d in range(1, chips):
                for c in range(CUTS):
                    far_copy(source, d, c).start()


    step_rows = rows_dev // CHUNKS

    def want(c):
        first_zone = jnp.where(owner, jnp.where(c * 2 < chips, NEAR0, FAR0), jnp.where(c * 2 < chips, NEAR1, FAR1))
        return jnp.where(zone == 0, first_zone, jnp.where(owner, jnp.where(zone < steps - 1, 1, 0), REST1))

    n_extra = want(chip)
    wants = [want((chip + d) % chips) for d in range(chips)]
    head = jnp.where(owner, HEAD0, HEAD1)

    def span(m):
        return pl.ds(pl.multiple_of(m * step_rows, step_rows), step_rows)

    def extra_copy(g, d):
        return remote(
            factors_hbm.at[span(CHUNKS - 1 - g)], extra.at[g, row], x_send.at[g, d], x_recv.at[g, row],
            row=far[d - 1] if d else sibling,
        )

    def extra_forward(g, source):
        return remote(extra.at[g, source], extra.at[g, source], x_fwd.at[g, source // 2], x_recv.at[g, source], row=sibling)

    def extra_start(g, carry):
        for d in range(chips):
            pl.when(g < wants[d])(lambda: extra_copy(g, d).start())
        return carry

    waits = jnp.logical_and(owner, zone > 0)
    sub = width // SUBS

    def batch(s, start=0):
        return pl.ds(pl.multiple_of(start + s * sub, sub), sub)

    def stacked(value):
        high, low = split(value)
        return high, jnp.concatenate([high, low])

    def folded(both, more):
        return both[:sub] + (both[sub:] + more)

    def solve_low(value):
        high, both = stacked(value)
        top = folded(dot_t(both[:, :half], low_hi[:half, :half]), dot_t(high[:, :half], low_lo[:half, :half]))
        return jnp.concatenate([top, folded(dot_t(both, low_hi[half:]), dot_t(high, low_lo[half:]))], axis=1)

    def solve_up(value):
        high, both = stacked(value)
        end = folded(dot_t(both[:, half:], up_hi[half:, half:]), dot_t(high[:, half:], up_lo[half:, half:]))
        return jnp.concatenate([folded(dot_t(both, up_hi[:half]), dot_t(high, up_lo[:half])), end], axis=1)

    def slot(t):
        return jnp.where(t <= zone, t, steps + zone - t)

    def is_far(source):
        return jnp.logical_and(owner, source // 2 != chip)

    def relay_panel(j):
        for p in range(pieces):
            source = j * pieces + p

            @pl.when(is_far(source))
            def _():
                for c in range(CUTS):
                    relay_copy(source, core, c).wait_recv()
                    relay_copy(source, core, c).start()

    def relay_back():
        def one(i, carry):
            relay_panel(steps - 1 - i)
            return carry

        lax.fori_loop(0, steps - 1 - zone, one, 0)

    def arrive_panel(j):
        for p in range(pieces):
            source = j * pieces + p

            @pl.when(source != row)
            def _():
                for c in range(CUTS):
                    relay_copy(source, 1 - core, c).wait_recv()

    def chain_copy(t, s):
        piece = solved.at[t, batch(s)]
        k = jnp.where(t == 0, 0, 1)
        return remote(
            piece, piece, s_chain.at[k, s], s_recv.at[t, s], col=jnp.minimum(zone + 1, steps - 1) * side
        )

    def chains(t):
        return jnp.logical_and(owner, jnp.logical_and((t == 0) | (t == zone), zone < steps - 1))

    def arrival(j, s):
        piece = solved.at[j, batch(s)]
        return remote(piece, piece, s_chain.at[0, s], s_recv.at[j, s], col=col)

    def help_copy(z, s):
        piece = solved.at[zone, batch(s)]
        return remote(piece, piece, s_help.at[z, s], s_recv.at[zone, s], col=z * side)

    def help_last(z, s):
        return remote(last.at[batch(s)], solved.at[zone, batch(s)], s_help.at[z, s], s_recv.at[zone, s], col=z * side)

    def hint_copy(d, s):
        return remote(last.at[batch(s)], last.at[batch(s)], s_hint.at[d, s], l_recv.at[s], col=base + d)

    def lane_last(s):
        return remote(last.at[batch(s)], solved.at[zone, batch(s)], s_chain.at[0, s], s_recv.at[zone, s], col=lane)

    def skip_last(s):
        target = jnp.maximum(zone - 2, 0) * side
        return remote(last.at[batch(s)], solved.at[zone, batch(s)], s_chain.at[2, s], s_recv.at[zone, s], col=target)

    def forwards(what, s):
        for z in range(2, steps):
            pl.when(jnp.logical_and(helper, jnp.logical_and(z > zone + 1, zone > 0)))(
                lambda: what(help_copy(z, s))
            )

    def backwards(what, s):
        for z in reversed(range(steps - 3)):
            pl.when(jnp.logical_and(helper, z < zone - 2))(lambda: what(help_last(z, s)))
        what(lane_last(s))

    def begin(copy):
        copy.start()

    def finished(copy):
        copy.wait_send()

    def side_copy(t, j, d, s):
        piece = solved.at[j, batch(s)]
        return remote(piece, piece, s_side.at[t, d, s], s_recv.at[j, s], col=base + d)

    def lends(t):
        return jnp.logical_and(zone == 0, t < steps)

    def row_copy(t, j, s, p):
        return remote(
            solved.at[j, batch(s), pl.ds(p * cols, cols)], gathered.at[core, batch(s, chip * width)],
            s_row.at[t, s, p], g_recv.at[row, s], row=j * pieces + p,
        )

    def local_copy(j, s, p):
        return pltpu.make_async_copy(
            solved.at[j, batch(s), pl.ds(p * cols, cols)], gathered.at[core, batch(s, chip * width)], g_local.at[s]
        )

    def shares(t, j, s, what):
        for p in range(pieces):
            target = j * pieces + p
            lent = jnp.logical_and(lends(t), target // 2 != chip)
            sends = jnp.logical_and(target != row, jnp.logical_or(owner, jnp.logical_not(lent)))
            pl.when(sends)(lambda: what(row_copy(t, j, s, p)))

    my_turn = jnp.where(row // pieces == 0, 0, steps - row // pieces)
    lender = jnp.logical_and(owner, lends(my_turn))

    def lend_copy(d, k, s):
        source = far[k // 2] // 2 * 2 + k % 2
        piece = gathered.at[k % 2, batch(s, (source // 2) * width)]
        return remote(piece, piece, s_lend.at[d, k, s], g_recv.at[source, s], col=base + d)

    def lend(s):
        for k in range(2 * (chips - 1)):
            lend_copy(1, k, s).wait_recv()
            for d in range(1, side):
                lend_copy(d, k, s).start()

    put_off = zone == steps - 1

    def has_sides(j):
        return jnp.logical_and(owner, jnp.logical_or(zone > 0, j < 2))

    def sides(t, j, s):
        for d in range(1, side):
            side_copy(t, j, d, s).start()

    def pass_on(t, j, s):
        pl.when(chains(t))(lambda: chain_copy(t, s).start())

        @pl.when(jnp.logical_and(has_sides(j), jnp.logical_not(jnp.logical_and(put_off, t < zone))))
        def _():
            sides(t, j, s)

        pl.when(t == zone)(lambda: forwards(begin, s))
        shares(t, j, s, begin)
        for p in range(pieces):
            pl.when(j * pieces + p == row)(lambda: local_copy(j, s, p).start())

    def update(j, s):
        total = state[batch(s)]
        for p in range(pieces):
            total = total - dot_t(solved[j, batch(s), pl.ds(p * cols, cols)], panel[j * pieces + p])
        state[batch(s)] = total

    def solve_first(s, sends=True):
        value = state[batch(s)]
        value = value + solve_low(value)
        state[batch(s)] = value
        solved[zone, batch(s)] = value.astype(BF16)
        if sends:
            pass_on(zone, zone, s)

    def last_copy(s):
        target = jnp.where(zone > 0, zone - 1, 0) * side
        return remote(last.at[batch(s)], solved.at[zone, batch(s)], s_last.at[s], s_recv.at[zone, s], col=target)

    def solve_last(s):
        value = solve_up(state[batch(s)])
        state[batch(s)] = value
        last[batch(s)] = value.astype(BF16)
        pl.when(zone > 0)(lambda: last_copy(s).start())

        @pl.when(zone > 1)
        def _():
            for d in range(1, side):
                hint_copy(d, s).start()


    def out_copy(m):
        return pltpu.make_async_copy(taken.at[span(m)], out_ref.at[span(m)], out_sem.at[m])

    def one_copy(m):
        return remote(send1.at[m], recv1.at[m], one_send.at[m], one_recv.at[m], row=sibling)

    def two_copy(m, d):
        return remote(send2.at[m, d - 1], recv2.at[m, d - 1], two_send.at[m, d - 1], two_recv.at[m, d - 1], row=far[d - 1])

    def first(m, carry):
        send1[m] = dot_t(factors_ref[span(m)], gathered[1 - core]).astype(BF16)
        one_copy(m).start()
        return carry

    def second(m, carry):
        @pl.when(m + 1 < n_made)
        def _():
            first(m + 1, 0)

        own1[m] = dot_t(factors_ref[span(m)], gathered[core])
        one_copy(m).wait_recv()
        for d in range(1, chips):
            there = pl.ds(pl.multiple_of(((chip + d) % chips) * width, width), width)

            @pl.when(m < CHUNKS - wants[d])
            def _():
                send2[m, d - 1] = (own1[m, :, there] + recv1[m, :, there].astype(F32)).astype(BF16)
                two_copy(m, d).start()

        return carry

    def third(m, carry):
        here = pl.ds(pl.multiple_of(chip * width, width), width)
        total = own1[m, :, here] + recv1[m, :, here].astype(F32)
        for d in range(1, chips):
            two_copy(m, d).wait_recv()
            total = total + recv2[m, d - 1].astype(F32)
        taken[span(m)] = total
        out_copy(m).start()
        return carry

    def finish(m, carry):
        one_copy(m).wait_send()
        for d in range(1, chips):
            pl.when(m < CHUNKS - wants[d])(lambda: two_copy(m, d).wait_send())
        return carry

    n_swap = CHUNKS - n_extra
    fewest = wants[0]
    for d in range(1, chips):
        fewest = jnp.minimum(fewest, wants[d])
    n_made = CHUNKS - fewest
    start = jnp.where(owner, block // step_rows, 0)

    def extra_hand_on(g, carry):
        for d in range(1, chips):
            extra_forward(g, far[d - 1]).wait_recv()
            extra_forward(g, far[d - 1]).start()
        return carry

    def extra_product(g, carry):
        rows = span(CHUNKS - 1 - g)
        total = jnp.zeros((step_rows, width), F32)
        for d in range(n_row):
            source = (row + d) % n_row
            part_of = solved[source // pieces, :, pl.ds(pl.multiple_of((source % pieces) * cols, cols), cols)]
            if d == 0:
                total = total + dot_t(factors_ref[rows], part_of)
            else:
                @pl.when(source % 2 != core)
                def _():
                    extra_forward(g, source).wait_recv()

                total = total + dot_t(extra[g, source], part_of)
        taken[rows] = total
        out_copy(CHUNKS - 1 - g).start()
        return carry

    def extra_finish(g, carry):
        for d in range(chips):
            pl.when(g < wants[d])(lambda: extra_copy(g, d).wait_send())

        @pl.when(g < n_extra)
        def _():
            for d in range(1, chips):
                extra_forward(g, far[d - 1]).wait_send()

        return carry

    def first_products():
        factors_copy.wait()
        rhs_copy.wait()

        def arrive(s, carry):
            local_copy(0, s, 0).wait()
            for d in range(1, n_row):
                source = (row + d) % n_row
                piece = gathered.at[source % 2, batch(s, (source // 2) * width)]
                taken_on = jnp.logical_and(lender, source // 2 != chip)
                arrived = remote(piece, piece, g_local.at[s], g_recv.at[source, s], row=source)
                pl.when(jnp.logical_not(taken_on))(arrived.wait_recv)
            return carry

        lax.fori_loop(0, SUBS, arrive, 0)
        first(start, 0)

    def batches(what):
        def one(s, carry):
            what(s)
            return carry

        lax.fori_loop(0, SUBS, one, 0)

    def prepare():
        diag_copy.wait()
        work_copy.wait()
        down = lax.broadcasted_iota(jnp.int32, (block, block), 0)
        across = lax.broadcasted_iota(jnp.int32, (block, block), 1)
        matrix = diag[...]
        low_hi[...], low_lo[...] = split(jnp.where(down > across, matrix, 0.0))
        up_hi[...], up_lo[...] = split(jnp.where(down <= across, matrix, 0.0))
        state[...] = work[...].T

    def products():
        first_products()
        lax.fori_loop(start, n_made, second, 0)

    final = slot(steps - 1) * pieces // 2
    sooner = jnp.logical_and(jnp.logical_not(owner), jnp.logical_and(zone == 0, final != chip))
    opens = jnp.logical_and(owner, zone == 0)

    @pl.when(opens)
    def _():
        prepare()
        batches(lambda s: solve_first(s, False))

    pl.semaphore_wait(barrier, n_row - 1 + jnp.where(owner, ends + side - 1, 1 + jnp.where(helper, beyond, 0)))
    @pl.when(sends_panel)
    def _():
        for h in (1 - core, core):
            for c in range(CUTS):
                near_copy(h, c).start()

    @pl.when(owner)
    def _():
        panel_own.wait()
        pl.when(leading == row)(lambda: far_sends(leading))

    pl.when(opens)(lambda: batches(lambda s: pass_on(zone, zone, s)))
    lax.fori_loop(0, jnp.where(owner, 0, head), extra_start, 0)
    pl.when(jnp.logical_and(owner, zone > 0))(prepare)
    factors_copy.start()
    rhs_copy.start()

    @pl.when(owner)
    def _():

        pl.when(leading != row)(lambda: far_sends(leading))
        far_sends(trailing)
        lax.fori_loop(0, jnp.where(zone == 0, head, 0), extra_start, 0)
        pl.when(zone == 0)(relay_back)

        def hop(i, carry):
            t = jnp.where(i < zone, i, i + 1)
            j = slot(t)

            late = jnp.logical_and(is_far(j * pieces), i < zone)

            def take(s):
                arrival(j, s).wait_recv()
                pass_on(t, j, s)

            @pl.when(late)
            def _():
                batches(take)
                relay_panel(j)

            def one(s):
                pl.when(jnp.logical_not(late))(lambda: take(s))
                pl.when(s == 0)(lambda: arrive_panel(j))
                update(j, s)
                pl.when(i + 1 == zone)(lambda: solve_first(s))
                pl.when(jnp.logical_and(i == steps - 2, zone > 0))(lambda: solve_last(s))

            batches(one)
            lax.fori_loop(0, jnp.where(jnp.logical_and(waits, i == 0), head, 0), extra_start, 0)
            lax.fori_loop(head, jnp.where(i == 1, GATHER, head), extra_start, 0)
            pl.when(i + 1 == zone)(relay_back)
            pl.when(jnp.logical_and(lender, i == jnp.maximum(my_turn - 1, 0)))(lambda: batches(lend))
            return carry

        lax.fori_loop(0, steps - 1, hop, 0)

        pl.when(zone > 1)(lambda: batches(lambda s: skip_last(s).start()))

        @pl.when(put_off)
        def _():
            for t in range(steps - 1):
                batches(lambda s: sides(t, t, s))

    @pl.when(jnp.logical_not(owner))
    def _():
        def hop(i, carry):
            t = jnp.where(put_off, (i + steps - 1) % steps, i)
            j = slot(t)

            def one(s):
                arrival(j, s).wait_recv()
                pass_on(t, j, s)

                @pl.when(jnp.logical_and(t == steps - 1, zone > 1))
                def _():
                    hint_copy(1, s).wait_recv()
                    backwards(begin, s)

            batches(one)
            lax.fori_loop(head, jnp.where(i == 2, GATHER, head), extra_start, 0)
            return carry

        def each(i, carry):
            pl.when(jnp.logical_and(sooner, i == steps - 1))(products)
            return hop(i, carry)

        lax.fori_loop(0, steps, each, 0)

    pl.when(jnp.logical_not(sooner))(products)
    lax.fori_loop(0, n_extra, extra_hand_on, 0)
    pl.when(jnp.logical_and(owner, zone == 0))(lambda: batches(solve_last))
    lax.fori_loop(0, n_extra, extra_product, 0)

    @pl.when(owner)
    def _():
        taken[pl.ds(0, block)] = rhs_ref[...] - state[...].T
        for m in range(block // step_rows):
            out_copy(m).start()

    lax.fori_loop(start, n_swap, third, 0)
    lax.fori_loop(start, n_made, finish, 0)
    lax.fori_loop(0, GATHER, extra_finish, 0)

    @pl.when(sends_panel)
    def _():
        for h in range(2):
            for c in range(CUTS):
                near_copy(h, c).wait_send()

    for source in (pair, pair + 1):
        @pl.when(needed(source))
        def _():
            for d in range(1, chips):
                for c in range(CUTS):
                    far_copy(source, d, c).wait_send()

    def written(m, carry):
        out_copy(m).wait()
        return carry

    def drain(t, carry):
        j = slot(t)

        for p in range(pieces):
            source = j * pieces + p

            @pl.when(jnp.logical_and(is_far(source), t != zone))
            def _():
                for c in range(CUTS):
                    relay_copy(source, core, c).wait_send()

        def one(s):
            pl.when(chains(t))(lambda: chain_copy(t, s).wait_send())
            pl.when(t == zone)(lambda: forwards(finished, s))

            @pl.when(has_sides(j))
            def _():
                for d in range(1, side):
                    side_copy(t, j, d, s).wait_send()

            shares(t, j, s, finished)

        batches(one)
        return carry

    lax.fori_loop(0, steps, drain, 0)

    lax.fori_loop(0, CHUNKS, written, 0)

    @pl.when(lender)
    def _():
        for d in range(1, side):
            for k in range(2 * (chips - 1)):
                batches(lambda s: lend_copy(d, k, s).wait_send())

    @pl.when(jnp.logical_and(owner, zone > 0))
    def _():
        batches(lambda s: last_copy(s).wait_send())

    @pl.when(jnp.logical_and(owner, zone > 1))
    def _():
        batches(lambda s: skip_last(s).wait_send())
        for d in range(1, side):
            batches(lambda s: hint_copy(d, s).wait_send())

    @pl.when(jnp.logical_and(jnp.logical_not(owner), zone > 1))
    def _():
        batches(lambda s: backwards(finished, s))


def body(rhs, factors, diag_inv):
    n_row, n_col = lax.axis_size("row"), lax.axis_size("col")
    rows_dev, width = rhs.shape
    cols = factors.shape[1]
    steps, block = diag_inv.shape[:2]
    pieces, chips, side = block // cols, n_row // 2, n_col // steps
    step_rows = rows_dev // CHUNKS
    dma = pltpu.SemaphoreType.DMA
    taken = pl.pallas_call(
        functools.partial(kernel, n_row, n_col, steps, block),
        out_shape=jax.ShapeDtypeStruct(rhs.shape, F32),
        in_specs=[pl.BlockSpec(memory_space=pl.ANY)] * 3,
        out_specs=pl.BlockSpec(memory_space=pl.ANY),
        scratch_shapes=[
            pltpu.VMEM((block, width), F32),
            pltpu.VMEM(factors.shape, BF16),
            pltpu.VMEM((GATHER, n_row, step_rows, cols), BF16),
            pltpu.VMEM(rhs.shape, F32),
            pltpu.VMEM((block, block), F32),
            pltpu.VMEM((block, block), BF16),
            pltpu.VMEM((block, block), BF16),
            pltpu.VMEM((block, block), BF16),
            pltpu.VMEM((block, block), BF16),
            pltpu.VMEM((n_row, block, cols), BF16),
            pltpu.VMEM((steps, width, block), BF16),
            pltpu.VMEM((width, block), BF16),
            pltpu.VMEM((block, width), F32),
            pltpu.VMEM((width, block), F32),
            pltpu.VMEM((2, chips * width, cols), BF16),
            pltpu.VMEM((CHUNKS, step_rows, chips * width), BF16),
            pltpu.VMEM((CHUNKS, step_rows, chips * width), BF16),
            pltpu.VMEM((CHUNKS, step_rows, chips * width), F32),
            pltpu.VMEM((CHUNKS, chips - 1, step_rows, width), BF16),
            pltpu.VMEM((CHUNKS, chips - 1, step_rows, width), BF16),
            dma, dma((2, CUTS)), dma((2, chips - 1, CUTS)), dma((n_row, 2, CUTS)), dma((n_row, CUTS)),
            dma((3, SUBS)), dma((steps, side, SUBS)), dma((steps, SUBS, pieces)), dma((side, 2 * (chips - 1), SUBS)),
            dma((steps, SUBS)), dma((side, SUBS)), dma((steps, SUBS)), dma((SUBS,)), dma((SUBS,)),
            dma((SUBS,)), dma((n_row, SUBS)),
            dma((CHUNKS,)), dma((CHUNKS,)), dma((CHUNKS, chips - 1)), dma((CHUNKS, chips - 1)),
            dma((GATHER, chips)), dma((GATHER, n_row)), dma((GATHER, chips)), dma((4,)), dma((CHUNKS,)),
        ],
        compiler_params=pltpu.CompilerParams(
            collective_id=0, has_side_effects=True, vmem_limit_bytes=50 * 1024 * 1024
        ),
    )(rhs, factors, diag_inv)
    return rhs - taken


def solution(mesh):
    placed = (P("col", "row"), P("col", "row"), P())
    return jax.shard_map(
        body, mesh=mesh, in_specs=placed, out_specs=P("col", "row"), check_vma=False
    )
```

```python
import functools

import jax
import jax.numpy as jnp
from jax import lax
from jax.experimental import pallas as pl
from jax.experimental.pallas import tpu as pltpu
from jax.sharding import PartitionSpec as P

MESH = pl.DeviceIdType.MESH
F32 = jnp.float32
BF16 = jnp.bfloat16
CHUNKS = 8
SUBS = 2
CUTS = 2
GATHER = 4
NEAR0, FAR0, NEAR1, FAR1, REST1 = 2, 3, 4, 4, 2
HEAD0, HEAD1 = 2, 4


def remote(src, dst, send_sem, recv_sem, **device):
    return pltpu.make_async_remote_copy(
        src_ref=src,
        dst_ref=dst,
        send_sem=send_sem,
        recv_sem=recv_sem,
        device_id=device,
        device_id_type=MESH,
    )


def dot(a, b):
    return jnp.dot(a, b, preferred_element_type=F32)


def dot_t(a, b):
    return lax.dot_general(a, b, (((1,), (1,)), ((), ())), preferred_element_type=F32)


def split(value):
    high = value.astype(BF16)
    return high, (value - high.astype(F32)).astype(BF16)


def kernel(
    n_row, n_col, steps, block,
    rhs_hbm, factors_hbm, diag_ref, out_ref,
    rhs_ref, factors_ref, extra, taken,
    diag, low_hi, low_lo, up_hi, up_lo, panel, solved, last, work, state, gathered,
    send1, recv1, own1, send2, recv2,
    diag_sem, f_send, f_far, f_recv, f_fwd, s_chain, s_side, s_row, s_lend, s_help, s_hint, s_recv, l_recv, s_last, g_local, g_recv,
    one_send, one_recv, two_send, two_recv, x_send, x_recv, x_fwd, load_sem, out_sem,
):
    rows_dev, width = rhs_hbm.shape
    cols = factors_ref.shape[1]
    pieces = block // cols
    chips = n_row // 2
    side = n_col // steps
    row = lax.axis_index("row")
    col = lax.axis_index("col")
    chip, core = row // 2, row % 2
    sibling = chip * 2 + 1 - core
    zone, lane = col // side, col % side
    owner = lane == 0
    helper = lane == 1
    base = zone * side

    diag_copy = pltpu.make_async_copy(diag_ref.at[zone], diag, diag_sem)
    rhs_copy = pltpu.make_async_copy(rhs_hbm, rhs_ref, load_sem.at[0])
    factors_copy = pltpu.make_async_copy(factors_hbm, factors_ref, load_sem.at[1])
    work_copy = pltpu.make_async_copy(rhs_hbm.at[pl.ds(0, block)], work, load_sem.at[2])
    panel_own = pltpu.make_async_copy(factors_hbm.at[pl.ds(0, block)], panel.at[row], load_sem.at[3])
    @pl.when(owner)
    def _():
        diag_copy.start()
        work_copy.start()
        panel_own.start()


    barrier = pltpu.get_barrier_semaphore()
    for d in range(1, n_row):
        pl.semaphore_signal(barrier, inc=1, device_id={"row": (row + d) % n_row}, device_id_type=MESH)

    def greet(other):
        pl.semaphore_signal(barrier, inc=1, device_id={"col": other}, device_id_type=MESH)

    @pl.when(owner)
    def _():
        for d in range(1, side):
            greet(base + d)

    pl.when(jnp.logical_and(owner, zone > 0))(lambda: greet(base - side))
    pl.when(jnp.logical_and(owner, zone < steps - 1))(lambda: greet(base + side))
    pl.when(jnp.logical_not(owner))(lambda: greet(base))
    for z in range(1, steps - 2):
        pl.when(jnp.logical_and(owner, zone > z + 1))(lambda: greet(z * side + 1))
    beyond = jnp.where(jnp.logical_and(zone > 0, zone < steps - 2), steps - 2 - zone, 0)
    ends = jnp.where(zone > 0, 1, 0) + jnp.where(zone < steps - 1, 1, 0)

    far = [((chip + d) % chips) * 2 + core for d in range(1, chips)]
    sends_panel = jnp.logical_and(owner, row // pieces != zone)
    half = block // 2
    cut_rows = half // CUTS
    pair = chip * 2
    later = pair // pieces > zone
    leading = jnp.where(later, pair + 1, pair)
    trailing = jnp.where(later, pair, pair + 1)

    def cut(h, c):
        return pl.ds(pl.multiple_of(h * half + c * cut_rows, cut_rows), cut_rows)

    def needed(source):
        return jnp.logical_and(owner, source // pieces != zone)

    def near_copy(mine, c):
        rows = cut(core if mine else 1 - core, c)
        there = f_recv.at[row, CUTS if mine else c]
        return remote(factors_hbm.at[rows], panel.at[row, rows], f_send, there, row=sibling)

    def far_copy(source, d, c):
        piece = panel.at[source, cut(core, c)]
        return remote(piece, piece, f_far.at[source % 2, d - 1], f_recv.at[source, c], row=far[d - 1])

    def arriving(source, c):
        piece = panel.at[source, cut(core, c)]
        return remote(piece, piece, f_fwd.at[source], f_recv.at[source, c], row=sibling)

    def relay_copy(source, c):
        piece = panel.at[source, cut(core, c)]
        return remote(piece, piece, f_fwd.at[source], f_recv.at[source, CUTS], row=sibling)

    def half_block(source, h):
        return panel.at[source, pl.ds(pl.multiple_of(h * half, half), half)]

    def far_sends(source):
        @pl.when(needed(source))
        def _():
            @pl.when(source != row)
            def _():
                for c in range(CUTS):
                    arriving(source, c).wait_recv()

            for d in range(1, chips):
                for c in range(CUTS):
                    far_copy(source, d, c).start()


    step_rows = rows_dev // CHUNKS

    def want(c):
        first_zone = jnp.where(owner, jnp.where(c * 2 < chips, NEAR0, FAR0), jnp.where(c * 2 < chips, NEAR1, FAR1))
        return jnp.where(zone == 0, first_zone, jnp.where(owner, jnp.where(zone < steps - 1, 1, 0), REST1))

    n_extra = want(chip)
    wants = [want((chip + d) % chips) for d in range(chips)]
    head = jnp.where(owner, HEAD0, HEAD1)

    def span(m):
        return pl.ds(pl.multiple_of(m * step_rows, step_rows), step_rows)

    def extra_copy(g, d):
        return remote(
            factors_hbm.at[span(CHUNKS - 1 - g)], extra.at[g, core, chip], x_send.at[g, d], x_recv.at[g, (chips - 1 if d == 0 else chips - 1 - d)],
            row=far[d - 1] if d else sibling,
        )

    def extra_arriving(g, d):
        piece = extra.at[g, core, far[d - 1] // 2]
        return remote(piece, piece, x_fwd.at[g, d - 1], x_recv.at[g, d - 1], row=sibling)

    def extra_forward(g, d):
        piece = extra.at[g, core, far[d - 1] // 2]
        return remote(piece, piece, x_fwd.at[g, d - 1], x_recv.at[g, chips - 1], row=sibling)

    def extra_start(g, carry):
        for d in range(chips):
            pl.when(g < wants[d])(lambda: extra_copy(g, d).start())
        return carry

    waits = jnp.logical_and(owner, zone > 0)
    sub = width // SUBS

    def batch(s, start=0):
        return pl.ds(pl.multiple_of(start + s * sub, sub), sub)

    def stacked(value):
        high, low = split(value)
        return high, jnp.concatenate([high, low])

    def folded(both, more):
        return both[:sub] + (both[sub:] + more)

    def solve_low(value):
        high, both = stacked(value)
        top = folded(dot_t(both[:, :half], low_hi[:half, :half]), dot_t(high[:, :half], low_lo[:half, :half]))
        return jnp.concatenate([top, folded(dot_t(both, low_hi[half:]), dot_t(high, low_lo[half:]))], axis=1)

    def solve_up(value):
        high, both = stacked(value)
        end = folded(dot_t(both[:, half:], up_hi[half:, half:]), dot_t(high[:, half:], up_lo[half:, half:]))
        return jnp.concatenate([folded(dot_t(both, up_hi[:half]), dot_t(high, up_lo[:half])), end], axis=1)

    def slot(t):
        return jnp.where(t <= zone, t, steps + zone - t)

    def is_far(source):
        return jnp.logical_and(owner, source // 2 != chip)

    def relay_panel(j):
        for p in range(pieces):
            source = j * pieces + p

            @pl.when(is_far(source))
            def _():
                for c in range(CUTS):
                    arriving(source, c).wait_recv()
                    relay_copy(source, c).start()

    def relay_back():
        def one(i, carry):
            relay_panel(steps - 1 - i)
            return carry

        lax.fori_loop(0, steps - 1 - zone, one, 0)

    def arrive_panel(j):
        for p in range(pieces):
            source = j * pieces + p

            @pl.when(source != row)
            def _():
                piece = half_block(source, 1 - core)
                remote(piece, piece, f_fwd.at[source], f_recv.at[source, CUTS], row=sibling).wait_recv()

    def chain_copy(t, s):
        piece = solved.at[t, batch(s)]
        k = jnp.where(t == 0, 0, 1)
        return remote(
            piece, piece, s_chain.at[k], s_recv.at[t, s], col=jnp.minimum(zone + 1, steps - 1) * side
        )

    def chains(t):
        return jnp.logical_and(owner, jnp.logical_and((t == 0) | (t == zone), zone < steps - 1))

    def arrival(j, s):
        piece = solved.at[j, batch(s)]
        return remote(piece, piece, s_chain.at[0], s_recv.at[j, s], col=col)

    def help_copy(z, s):
        piece = solved.at[zone, batch(s)]
        return remote(piece, piece, s_help.at[z], s_recv.at[zone, s], col=z * side)

    def help_last(z, s):
        return remote(last.at[batch(s)], solved.at[zone, batch(s)], s_help.at[z], s_recv.at[zone, s], col=z * side)

    def hint_copy(d, s):
        return remote(last.at[batch(s)], last.at[batch(s)], s_hint.at[d - 1], l_recv.at[s], col=base + d)

    def lane_last(s):
        return remote(last.at[batch(s)], solved.at[zone, batch(s)], s_chain.at[0], s_recv.at[zone, s], col=lane)

    def skip_last(s):
        target = jnp.maximum(zone - 2, 0) * side
        return remote(last.at[batch(s)], solved.at[zone, batch(s)], s_chain.at[2], s_recv.at[zone, s], col=target)

    def helps(z):
        return jnp.logical_and(helper, jnp.logical_and(z > zone + 1, zone > 0))

    def helps_back(z):
        return jnp.logical_and(helper, z < zone - 2)

    def forwards(s):
        for z in range(2, steps):
            pl.when(helps(z))(lambda: help_copy(z, s).start())

    def backwards(s):
        for z in reversed(range(steps - 3)):
            pl.when(helps_back(z))(lambda: help_last(z, s).start())
        lane_last(s).start()

    def side_copy(t, j, d, s):
        piece = solved.at[j, batch(s)]
        return remote(piece, piece, s_side.at[t, d - 1], s_recv.at[j, s], col=base + d)

    def lends(t):
        return jnp.logical_and(zone == 0, t < steps)

    def row_copy(t, j, s, p):
        return remote(
            solved.at[j, batch(s), pl.ds(p * cols, cols)], gathered.at[core, batch(s, chip * width)],
            s_row.at[t, p], g_recv.at[row, s], row=j * pieces + p,
        )

    def local_copy(j, s, p):
        return pltpu.make_async_copy(
            solved.at[j, batch(s), pl.ds(p * cols, cols)], gathered.at[core, batch(s, chip * width)], g_local.at[s]
        )

    def shares_with(t, j, p):
        target = j * pieces + p
        lent = jnp.logical_and(lends(t), target // 2 != chip)
        return jnp.logical_and(target != row, jnp.logical_or(owner, jnp.logical_not(lent)))

    my_turn = jnp.where(row // pieces == 0, 0, steps - row // pieces)
    lender = jnp.logical_and(owner, lends(my_turn))

    def lend_copy(d, k, s):
        source = far[k // 2] // 2 * 2 + k % 2
        piece = gathered.at[k % 2, batch(s, (source // 2) * width)]
        return remote(piece, piece, s_lend.at[d - 1, k], g_recv.at[source, s], col=base + d)

    def lend(s):
        for k in range(2 * (chips - 1)):
            lend_copy(1, k, s).wait_recv()
            for d in range(1, side):
                lend_copy(d, k, s).start()

    put_off = zone == steps - 1

    def has_sides(j):
        return jnp.logical_and(owner, jnp.logical_or(zone > 0, j < 2))

    def sent(piece, sem):
        remote(piece, piece, sem, sem, col=col).wait_send()

    def sides(t, j, s):
        for d in range(1, side):
            side_copy(t, j, d, s).start()

    def pass_on(t, j, s):
        pl.when(chains(t))(lambda: chain_copy(t, s).start())

        @pl.when(jnp.logical_and(has_sides(j), jnp.logical_not(jnp.logical_and(put_off, t < zone))))
        def _():
            sides(t, j, s)

        pl.when(t == zone)(lambda: forwards(s))
        for p in range(pieces):
            pl.when(shares_with(t, j, p))(lambda: row_copy(t, j, s, p).start())
            pl.when(j * pieces + p == row)(lambda: local_copy(j, s, p).start())

    def update(j, s):
        total = state[batch(s)]
        for p in range(pieces):
            total = total - dot_t(solved[j, batch(s), pl.ds(p * cols, cols)], panel[j * pieces + p])
        state[batch(s)] = total

    def solve_first(s, sends=True):
        value = state[batch(s)]
        value = value + solve_low(value)
        state[batch(s)] = value
        solved[zone, batch(s)] = value.astype(BF16)
        if sends:
            pass_on(zone, zone, s)

    def last_copy(s):
        target = jnp.where(zone > 0, zone - 1, 0) * side
        return remote(last.at[batch(s)], solved.at[zone, batch(s)], s_last, s_recv.at[zone, s], col=target)

    def solve_last(s):
        value = solve_up(state[batch(s)])
        state[batch(s)] = value
        last[batch(s)] = value.astype(BF16)
        pl.when(zone > 0)(lambda: last_copy(s).start())

        @pl.when(zone > 1)
        def _():
            for d in range(1, side):
                hint_copy(d, s).start()


    def out_copy(m):
        return pltpu.make_async_copy(taken.at[span(m)], out_ref.at[span(m)], out_sem)

    def one_copy(m):
        return remote(send1.at[m], recv1.at[m], one_send.at[m % 2], one_recv.at[m], row=sibling)

    def two_copy(m, d):
        return remote(send2.at[m, d - 1], recv2.at[m, d - 1], two_send.at[m, d - 1], two_recv.at[m, d - 1], row=far[d - 1])

    def first(m, carry):
        send1[m] = dot_t(factors_ref[span(m)], gathered[1 - core]).astype(BF16)
        pl.when(m > start + 1)(lambda: one_copy(m - 2).wait_send())
        one_copy(m).start()
        return carry

    def second(m, carry):
        @pl.when(m + 1 < n_made)
        def _():
            first(m + 1, 0)

        own1[m] = dot_t(factors_ref[span(m)], gathered[core])
        one_copy(m).wait_recv()
        for d in range(1, chips):
            there = pl.ds(pl.multiple_of(((chip + d) % chips) * width, width), width)

            @pl.when(m < CHUNKS - wants[d])
            def _():
                send2[m, d - 1] = (own1[m, :, there] + recv1[m, :, there].astype(F32)).astype(BF16)
                two_copy(m, d).start()

        return carry

    def third(m, carry):
        here = pl.ds(pl.multiple_of(chip * width, width), width)
        total = own1[m, :, here] + recv1[m, :, here].astype(F32)
        for d in range(1, chips):
            two_copy(m, d).wait_recv()
            total = total + recv2[m, d - 1].astype(F32)
        taken[span(m)] = rhs_ref[span(m)] - total
        out_copy(m).start()
        return carry

    def finish(m, carry):
        pl.when(m > n_made - 3)(lambda: one_copy(m).wait_send())
        for d in range(1, chips):
            pl.when(m < CHUNKS - wants[d])(lambda: two_copy(m, d).wait_send())
        return carry

    n_swap = CHUNKS - n_extra
    fewest = wants[0]
    for d in range(1, chips):
        fewest = jnp.minimum(fewest, wants[d])
    n_made = CHUNKS - fewest
    start = jnp.where(owner, block // step_rows, 0)

    def extra_hand_on(g, carry):
        for d in range(1, chips):
            extra_arriving(g, d).wait_recv()
            extra_forward(g, d).start()
        return carry

    def far_of(d):
        return ((chip + d) % chips) * 2 + core

    def extra_product(g, carry):
        rows = span(CHUNKS - 1 - g)
        total = jnp.zeros((step_rows, width), F32)
        theirs = extra.at[g, 1 - core]
        for d in range(n_row):
            source = far_of(d) if d < chips else (far_of(d - chips) // 2) * 2 + 1 - core
            part_of = solved[source // pieces, :, pl.ds(pl.multiple_of((source % pieces) * cols, cols), cols)]
            if d == 0:
                total = total + dot_t(factors_ref[rows], part_of)
            else:
                if d == chips:
                    remote(theirs, theirs, x_fwd.at[g, 0], x_recv.at[g, chips - 1], row=sibling).wait_recv()
                total = total + dot_t(extra[g, source % 2, source // 2], part_of)
        taken[rows] = rhs_ref[rows] - total
        out_copy(CHUNKS - 1 - g).start()
        return carry

    def extra_finish(g, carry):
        for d in range(chips):
            pl.when(g < wants[d])(lambda: extra_copy(g, d).wait_send())

        @pl.when(g < n_extra)
        def _():
            for d in range(1, chips):
                extra_forward(g, d).wait_send()

        return carry

    def first_products():
        factors_copy.wait()
        rhs_copy.wait()

        def arrive(s, carry):
            local_copy(0, s, 0).wait()
            for d in range(1, n_row):
                source = (row + d) % n_row
                piece = gathered.at[source % 2, batch(s, (source // 2) * width)]
                taken_on = jnp.logical_and(lender, source // 2 != chip)
                arrived = remote(piece, piece, g_local.at[s], g_recv.at[source, s], row=source)
                pl.when(jnp.logical_not(taken_on))(arrived.wait_recv)
            return carry

        lax.fori_loop(0, SUBS, arrive, 0)
        first(start, 0)

    def batches(what):
        def one(s, carry):
            what(s)
            return carry

        lax.fori_loop(0, SUBS, one, 0)

    def prepare():
        diag_copy.wait()
        work_copy.wait()
        down = lax.broadcasted_iota(jnp.int32, (block, block), 0)
        across = lax.broadcasted_iota(jnp.int32, (block, block), 1)
        matrix = diag[...]
        low_hi[...], low_lo[...] = split(jnp.where(down > across, matrix, 0.0))
        up_hi[...], up_lo[...] = split(jnp.where(down <= across, matrix, 0.0))
        state[...] = work[...].T

    def products():
        first_products()
        lax.fori_loop(start, n_made, second, 0)

    final = slot(steps - 1) * pieces // 2
    sooner = jnp.logical_and(jnp.logical_not(owner), jnp.logical_and(zone == 0, final != chip))
    opens = jnp.logical_and(owner, zone == 0)

    @pl.when(opens)
    def _():
        prepare()
        batches(lambda s: solve_first(s, False))

    pl.semaphore_wait(barrier, n_row - 1 + jnp.where(owner, ends + side - 1, 1 + jnp.where(helper, beyond, 0)))
    @pl.when(sends_panel)
    def _():
        for mine in (False, True):
            for c in range(CUTS):
                near_copy(mine, c).start()

    @pl.when(owner)
    def _():
        panel_own.wait()
        pl.when(leading == row)(lambda: far_sends(leading))

    pl.when(opens)(lambda: batches(lambda s: pass_on(zone, zone, s)))
    lax.fori_loop(0, jnp.where(owner, 0, head), extra_start, 0)
    pl.when(jnp.logical_and(owner, zone > 0))(prepare)
    factors_copy.start()
    rhs_copy.start()

    @pl.when(owner)
    def _():

        pl.when(leading != row)(lambda: far_sends(leading))
        far_sends(trailing)
        lax.fori_loop(0, jnp.where(zone == 0, head, 0), extra_start, 0)
        pl.when(zone == 0)(relay_back)

        def hop(i, carry):
            t = jnp.where(i < zone, i, i + 1)
            j = slot(t)

            late = jnp.logical_and(is_far(j * pieces), i < zone)

            def take(s):
                arrival(j, s).wait_recv()
                pass_on(t, j, s)

            @pl.when(late)
            def _():
                batches(take)
                relay_panel(j)

            def one(s):
                pl.when(jnp.logical_not(late))(lambda: take(s))
                pl.when(s == 0)(lambda: arrive_panel(j))
                update(j, s)
                pl.when(i + 1 == zone)(lambda: solve_first(s))
                pl.when(jnp.logical_and(i == steps - 2, zone > 0))(lambda: solve_last(s))

            batches(one)
            lax.fori_loop(0, jnp.where(jnp.logical_and(waits, i == 0), head, 0), extra_start, 0)
            lax.fori_loop(head, jnp.where(i == 1, GATHER, head), extra_start, 0)
            pl.when(i + 1 == zone)(relay_back)
            pl.when(jnp.logical_and(lender, i == jnp.maximum(my_turn - 1, 0)))(lambda: batches(lend))
            return carry

        lax.fori_loop(0, steps - 1, hop, 0)

        pl.when(zone > 1)(lambda: batches(lambda s: skip_last(s).start()))

        @pl.when(put_off)
        def _():
            for t in range(steps - 1):
                batches(lambda s: sides(t, t, s))

    @pl.when(jnp.logical_not(owner))
    def _():
        def hop(i, carry):
            t = jnp.where(put_off, (i + steps - 1) % steps, i)
            j = slot(t)

            def one(s):
                arrival(j, s).wait_recv()
                pass_on(t, j, s)

                @pl.when(jnp.logical_and(t == steps - 1, zone > 1))
                def _():
                    hint_copy(1, s).wait_recv()
                    backwards(s)

            batches(one)
            lax.fori_loop(head, jnp.where(i == 2, GATHER, head), extra_start, 0)
            return carry

        def each(i, carry):
            pl.when(jnp.logical_and(sooner, i == steps - 1))(products)
            return hop(i, carry)

        lax.fori_loop(0, steps, each, 0)

    pl.when(jnp.logical_not(sooner))(products)
    lax.fori_loop(0, n_extra, extra_hand_on, 0)
    pl.when(jnp.logical_and(owner, zone == 0))(lambda: batches(solve_last))
    lax.fori_loop(0, n_extra, extra_product, 0)

    @pl.when(owner)
    def _():
        taken[pl.ds(0, block)] = state[...].T
        for m in range(block // step_rows):
            out_copy(m).start()

    lax.fori_loop(start, n_swap, third, 0)
    lax.fori_loop(start, n_made, finish, 0)
    lax.fori_loop(0, GATHER, extra_finish, 0)

    @pl.when(sends_panel)
    def _():
        sent(panel.at[row], f_send)

    for source in (pair, pair + 1):
        @pl.when(needed(source))
        def _():
            for d in range(1, chips):
                sent(half_block(source, core), f_far.at[source % 2, d - 1])

    def drain(t, carry):
        j = slot(t)

        for p in range(pieces):
            source = j * pieces + p

            @pl.when(jnp.logical_and(is_far(source), t != zone))
            def _():
                sent(half_block(source, core), f_fwd.at[source])

        pl.when(chains(t))(lambda: sent(solved.at[t], s_chain.at[jnp.where(t == 0, 0, 1)]))

        @pl.when(t == zone)
        def _():
            for z in range(2, steps):
                pl.when(helps(z))(lambda: sent(solved.at[zone], s_help.at[z]))

        @pl.when(has_sides(j))
        def _():
            for d in range(1, side):
                sent(solved.at[j], s_side.at[t, d - 1])

        for p in range(pieces):
            pl.when(shares_with(t, j, p))(lambda: sent(gathered.at[0, pl.ds(0, width)], s_row.at[t, p]))

        return carry

    lax.fori_loop(0, steps, drain, 0)

    pltpu.make_async_copy(taken, out_ref, out_sem).wait()

    @pl.when(lender)
    def _():
        for d in range(1, side):
            for k in range(2 * (chips - 1)):
                sent(gathered.at[0, pl.ds(0, width)], s_lend.at[d - 1, k])

    pl.when(jnp.logical_and(owner, zone > 0))(lambda: sent(last, s_last))

    @pl.when(jnp.logical_and(owner, zone > 1))
    def _():
        sent(last, s_chain.at[2])
        for d in range(1, side):
            sent(last, s_hint.at[d - 1])

    @pl.when(jnp.logical_and(jnp.logical_not(owner), zone > 1))
    def _():
        sent(last, s_chain.at[0])
        for z in range(steps - 3):
            pl.when(helps_back(z))(lambda: sent(last, s_help.at[z]))


def body(rhs, factors, diag_inv):
    n_row, n_col = lax.axis_size("row"), lax.axis_size("col")
    rows_dev, width = rhs.shape
    cols = factors.shape[1]
    steps, block = diag_inv.shape[:2]
    pieces, chips, side = block // cols, n_row // 2, n_col // steps
    step_rows = rows_dev // CHUNKS
    dma = pltpu.SemaphoreType.DMA
    taken = pl.pallas_call(
        functools.partial(kernel, n_row, n_col, steps, block),
        out_shape=jax.ShapeDtypeStruct(rhs.shape, F32),
        in_specs=[pl.BlockSpec(memory_space=pl.ANY)] * 3,
        out_specs=pl.BlockSpec(memory_space=pl.ANY),
        scratch_shapes=[
            pltpu.VMEM(rhs.shape, F32),
            pltpu.VMEM(factors.shape, BF16),
            pltpu.VMEM((GATHER, 2, chips, step_rows, cols), BF16),
            pltpu.VMEM(rhs.shape, F32),
            pltpu.VMEM((block, block), F32),
            pltpu.VMEM((block, block), BF16),
            pltpu.VMEM((block, block), BF16),
            pltpu.VMEM((block, block), BF16),
            pltpu.VMEM((block, block), BF16),
            pltpu.VMEM((n_row, block, cols), BF16),
            pltpu.VMEM((steps, width, block), BF16),
            pltpu.VMEM((width, block), BF16),
            pltpu.VMEM((block, width), F32),
            pltpu.VMEM((width, block), F32),
            pltpu.VMEM((2, chips * width, cols), BF16),
            pltpu.VMEM((CHUNKS, step_rows, chips * width), BF16),
            pltpu.VMEM((CHUNKS, step_rows, chips * width), BF16),
            pltpu.VMEM((CHUNKS, step_rows, chips * width), F32),
            pltpu.VMEM((CHUNKS, chips - 1, step_rows, width), BF16),
            pltpu.VMEM((CHUNKS, chips - 1, step_rows, width), BF16),
            dma, dma, dma((2, chips - 1)), dma((n_row, CUTS + 1)), dma((n_row,)),
            dma((3,)), dma((steps, side - 1)), dma((steps, pieces)), dma((side - 1, 2 * (chips - 1))),
            dma((steps,)), dma((side - 1,)), dma((steps, SUBS)), dma((SUBS,)), dma,
            dma((SUBS,)), dma((n_row, SUBS)),
            dma((2,)), dma((CHUNKS,)), dma((CHUNKS, chips - 1)), dma((CHUNKS, chips - 1)),
            dma((GATHER, chips)), dma((GATHER, chips)), dma((GATHER, chips - 1)), dma((4,)), dma,
        ],
        compiler_params=pltpu.CompilerParams(
            collective_id=0, has_side_effects=True, vmem_limit_bytes=50 * 1024 * 1024
        ),
    )(rhs, factors, diag_inv)
    return taken


def solution(mesh):
    placed = (P("col", "row"), P("col", "row"), P())
    return jax.shard_map(
        body, mesh=mesh, in_specs=placed, out_specs=P("col", "row"), check_vma=False
    )
```

```python
import functools

import jax
import jax.numpy as jnp
from jax import lax
from jax.experimental import pallas as pl
from jax.experimental.pallas import tpu as pltpu
from jax.sharding import PartitionSpec as P

MESH = pl.DeviceIdType.MESH
F32 = jnp.float32
BF16 = jnp.bfloat16
CHUNKS = 8
SUBS = 2
CUTS = 2
GATHER = 4
NEAR0, FAR0, NEAR1, FAR1, REST1 = 2, 3, 4, 4, 2
HEAD0, HEAD1 = 2, 4
AHEAD = 3


def remote(src, dst, send_sem, recv_sem, **device):
    return pltpu.make_async_remote_copy(
        src_ref=src,
        dst_ref=dst,
        send_sem=send_sem,
        recv_sem=recv_sem,
        device_id=device,
        device_id_type=MESH,
    )


def dot(a, b):
    return jnp.dot(a, b, preferred_element_type=F32)


def dot_t(a, b):
    return lax.dot_general(a, b, (((1,), (1,)), ((), ())), preferred_element_type=F32)


def split(value):
    high = value.astype(BF16)
    return high, (value - high.astype(F32)).astype(BF16)


def kernel(
    n_row, n_col, steps, block,
    rhs_hbm, factors_hbm, diag_ref, out_ref,
    rhs_ref, factors_ref, extra, taken,
    diag, low, up, scale, panel, solved, last, work, state, gathered,
    send1, recv1, own1, send2, recv2,
    diag_sem, f_send, f_far, f_recv, f_fwd, s_chain, s_side, s_row, s_lend, s_help, s_hint, s_recv, l_recv, s_last, g_local, g_recv,
    one_send, one_recv, two_send, two_recv, x_send, x_recv, x_fwd, load_sem, out_sem,
):
    rows_dev, width = rhs_hbm.shape
    cols = factors_ref.shape[1]
    pieces = block // cols
    chips = n_row // 2
    side = n_col // steps
    row = lax.axis_index("row")
    col = lax.axis_index("col")
    chip, core = row // 2, row % 2
    sibling = chip * 2 + 1 - core
    zone, lane = col // side, col % side
    owner = lane == 0
    helper = lane == 1
    base = zone * side

    diag_copy = pltpu.make_async_copy(diag_ref.at[zone], diag, diag_sem)
    rhs_copy = pltpu.make_async_copy(rhs_hbm, rhs_ref, load_sem.at[0])
    factors_copy = pltpu.make_async_copy(factors_hbm, factors_ref, load_sem.at[1])
    work_copy = pltpu.make_async_copy(rhs_hbm.at[pl.ds(0, block)], work, load_sem.at[2])
    panel_own = pltpu.make_async_copy(factors_hbm.at[pl.ds(0, block)], panel.at[row], load_sem.at[3])
    @pl.when(owner)
    def _():
        diag_copy.start()
        work_copy.start()
        panel_own.start()


    barrier = pltpu.get_barrier_semaphore()
    for d in range(1, n_row):
        pl.semaphore_signal(barrier, inc=1, device_id={"row": (row + d) % n_row}, device_id_type=MESH)

    def greet(other):
        pl.semaphore_signal(barrier, inc=1, device_id={"col": other}, device_id_type=MESH)

    @pl.when(owner)
    def _():
        for d in range(1, side):
            greet(base + d)

    pl.when(jnp.logical_and(owner, zone > 0))(lambda: greet(base - side))
    pl.when(jnp.logical_and(owner, zone < steps - 1))(lambda: greet(base + side))
    pl.when(jnp.logical_not(owner))(lambda: greet(base))
    for z in range(1, steps - 2):
        pl.when(jnp.logical_and(owner, zone > z + 1))(lambda: greet(z * side + 1))
    beyond = jnp.where(jnp.logical_and(zone > 0, zone < steps - 2), steps - 2 - zone, 0)
    ends = jnp.where(zone > 0, 1, 0) + jnp.where(zone < steps - 1, 1, 0)

    far = [((chip + d) % chips) * 2 + core for d in range(1, chips)]
    sends_panel = jnp.logical_and(owner, row // pieces != zone)
    half = block // 2
    cut_rows = half // CUTS
    pair = chip * 2
    later = pair // pieces > zone
    leading = jnp.where(later, pair + 1, pair)
    trailing = jnp.where(later, pair, pair + 1)

    def cut(h, c):
        return pl.ds(pl.multiple_of(h * half + c * cut_rows, cut_rows), cut_rows)

    def needed(source):
        return jnp.logical_and(owner, source // pieces != zone)

    def near_copy(mine, c):
        rows = cut(core if mine else 1 - core, c)
        there = f_recv.at[row, CUTS if mine else c]
        return remote(factors_hbm.at[rows], panel.at[row, rows], f_send, there, row=sibling)

    def far_copy(source, d, c):
        piece = panel.at[source, cut(core, c)]
        return remote(piece, piece, f_far.at[source % 2, d - 1], f_recv.at[source, c], row=far[d - 1])

    def arriving(source, c):
        piece = panel.at[source, cut(core, c)]
        return remote(piece, piece, f_fwd.at[source], f_recv.at[source, c], row=sibling)

    def relay_copy(source, c):
        piece = panel.at[source, cut(core, c)]
        return remote(piece, piece, f_fwd.at[source], f_recv.at[source, CUTS], row=sibling)

    def half_block(source, h):
        return panel.at[source, pl.ds(pl.multiple_of(h * half, half), half)]

    def far_sends(source):
        @pl.when(needed(source))
        def _():
            @pl.when(source != row)
            def _():
                for c in range(CUTS):
                    arriving(source, c).wait_recv()

            for d in range(1, chips):
                for c in range(CUTS):
                    far_copy(source, d, c).start()


    step_rows = rows_dev // CHUNKS

    def want(c):
        first_zone = jnp.where(owner, jnp.where(c * 2 < chips, NEAR0, FAR0), jnp.where(c * 2 < chips, NEAR1, FAR1))
        return jnp.where(zone == 0, first_zone, jnp.where(owner, jnp.where(zone < steps - 1, 1, 0), REST1))

    n_extra = want(chip)
    wants = [want((chip + d) % chips) for d in range(chips)]
    head = jnp.where(owner, HEAD0, HEAD1)

    def span(m):
        return pl.ds(pl.multiple_of(m * step_rows, step_rows), step_rows)

    def extra_copy(g, d):
        return remote(
            factors_hbm.at[span(CHUNKS - 1 - g)], extra.at[g, core, chip], x_send.at[g, d], x_recv.at[g, (chips - 1 if d == 0 else chips - 1 - d)],
            row=far[d - 1] if d else sibling,
        )

    def extra_arriving(g, d):
        piece = extra.at[g, core, far[d - 1] // 2]
        return remote(piece, piece, x_fwd.at[g, d - 1], x_recv.at[g, d - 1], row=sibling)

    def extra_forward(g, d):
        piece = extra.at[g, core, far[d - 1] // 2]
        return remote(piece, piece, x_fwd.at[g, d - 1], x_recv.at[g, chips - 1], row=sibling)

    def extra_start(g, carry):
        for d in range(chips):
            pl.when(g < wants[d])(lambda: extra_copy(g, d).start())
        return carry

    waits = jnp.logical_and(owner, zone > 0)
    sub = width // SUBS

    def batch(s, start=0):
        return pl.ds(pl.multiple_of(start + s * sub, sub), sub)

    def stacked(value):
        return value.astype(BF16)

    def folded(both):
        return both

    def solve_low(value):
        both = stacked(value)
        top = folded(dot_t(both[:, :half], low[:half, :half]))
        return jnp.concatenate([top, folded(dot_t(both, low[half:]))], axis=1)

    def solve_up(value):
        both = stacked(value)
        end = folded(dot_t(both[:, half:], up[half:, half:]))
        return value * scale[...] + jnp.concatenate([folded(dot_t(both, up[:half])), end], axis=1)

    def slot(t):
        return jnp.where(t <= zone, t, steps + zone - t)

    def is_far(source):
        return jnp.logical_and(owner, source // 2 != chip)

    def relay_panel(j):
        for p in range(pieces):
            source = j * pieces + p

            @pl.when(is_far(source))
            def _():
                for c in range(CUTS):
                    arriving(source, c).wait_recv()
                    relay_copy(source, c).start()

    def relay_back():
        def one(i, carry):
            relay_panel(steps - 1 - i)
            return carry

        lax.fori_loop(0, steps - 1 - zone, one, 0)

    def arrive_panel(j):
        for p in range(pieces):
            source = j * pieces + p

            @pl.when(source != row)
            def _():
                piece = half_block(source, 1 - core)
                remote(piece, piece, f_fwd.at[source], f_recv.at[source, CUTS], row=sibling).wait_recv()

    def chain_copy(t, s):
        piece = solved.at[t, batch(s)]
        k = jnp.where(t == 0, 0, 1)
        return remote(
            piece, piece, s_chain.at[k], s_recv.at[t, s], col=jnp.minimum(zone + 1, steps - 1) * side
        )

    def chains(t):
        return jnp.logical_and(owner, jnp.logical_and((t == 0) | (t == zone), zone < steps - 1))

    def arrival(j, s):
        piece = solved.at[j, batch(s)]
        return remote(piece, piece, s_chain.at[0], s_recv.at[j, s], col=col)

    def help_copy(z, s):
        piece = solved.at[zone, batch(s)]
        return remote(piece, piece, s_help.at[z], s_recv.at[zone, s], col=z * side)

    def help_last(z, s):
        return remote(last.at[batch(s)], solved.at[zone, batch(s)], s_help.at[z], s_recv.at[zone, s], col=z * side)

    def hint_copy(d, s):
        return remote(last.at[batch(s)], last.at[batch(s)], s_hint.at[d - 1], l_recv.at[s], col=base + d)

    def lane_last(s):
        return remote(last.at[batch(s)], solved.at[zone, batch(s)], s_chain.at[0], s_recv.at[zone, s], col=lane)

    def skip_last(s):
        target = jnp.maximum(zone - 2, 0) * side
        return remote(last.at[batch(s)], solved.at[zone, batch(s)], s_chain.at[2], s_recv.at[zone, s], col=target)

    def helps(z):
        return jnp.logical_and(helper, jnp.logical_and(z > zone + 1, zone > 0))

    def helps_back(z):
        return jnp.logical_and(helper, z < zone - 2)

    def forwards(s):
        for z in range(2, steps):
            pl.when(helps(z))(lambda: help_copy(z, s).start())

    def backwards(s):
        for z in reversed(range(steps - 3)):
            pl.when(helps_back(z))(lambda: help_last(z, s).start())
        lane_last(s).start()

    def side_copy(t, j, d, s):
        piece = solved.at[j, batch(s)]
        return remote(piece, piece, s_side.at[t, d - 1], s_recv.at[j, s], col=base + d)

    def lends(t):
        return jnp.logical_and(zone == 0, t < steps)

    def row_copy(t, j, s, p):
        return remote(
            solved.at[j, batch(s), pl.ds(p * cols, cols)], gathered.at[core, batch(s, chip * width)],
            s_row.at[t, p], g_recv.at[row, s], row=j * pieces + p,
        )

    def local_copy(j, s, p):
        return pltpu.make_async_copy(
            solved.at[j, batch(s), pl.ds(p * cols, cols)], gathered.at[core, batch(s, chip * width)], g_local.at[s]
        )

    def shares_with(t, j, p):
        target = j * pieces + p
        lent = jnp.logical_and(lends(t), target // 2 != chip)
        return jnp.logical_and(target != row, jnp.logical_or(owner, jnp.logical_not(lent)))

    my_turn = jnp.where(row // pieces == 0, 0, steps - row // pieces)
    lender = jnp.logical_and(owner, lends(my_turn))

    def lend_copy(d, k, s):
        source = far[k // 2] // 2 * 2 + k % 2
        piece = gathered.at[k % 2, batch(s, (source // 2) * width)]
        return remote(piece, piece, s_lend.at[d - 1, k], g_recv.at[source, s], col=base + d)

    def lend(s):
        for k in range(2 * (chips - 1)):
            lend_copy(1, k, s).wait_recv()
            for d in range(1, side):
                lend_copy(d, k, s).start()

    put_off = zone == steps - 1

    def has_sides(j):
        return jnp.logical_and(owner, jnp.logical_or(zone > 0, j < 2))

    def sent(piece, sem):
        remote(piece, piece, sem, sem, col=col).wait_send()

    def sides(t, j, s):
        for d in range(1, side):
            side_copy(t, j, d, s).start()

    def pass_on(t, j, s):
        pl.when(chains(t))(lambda: chain_copy(t, s).start())

        @pl.when(jnp.logical_and(has_sides(j), jnp.logical_not(jnp.logical_and(put_off, t < zone))))
        def _():
            sides(t, j, s)

        pl.when(t == zone)(lambda: forwards(s))
        for p in range(pieces):
            pl.when(shares_with(t, j, p))(lambda: row_copy(t, j, s, p).start())
            pl.when(j * pieces + p == row)(lambda: local_copy(j, s, p).start())

    def update(j, s):
        total = state[batch(s)]
        for p in range(pieces):
            total = total - dot_t(solved[j, batch(s), pl.ds(p * cols, cols)], panel[j * pieces + p])
        state[batch(s)] = total

    def solve_first(s, sends=True):
        value = state[batch(s)]
        value = value + solve_low(value)
        state[batch(s)] = value
        solved[zone, batch(s)] = value.astype(BF16)
        if sends:
            pass_on(zone, zone, s)

    def last_copy(s):
        target = jnp.where(zone > 0, zone - 1, 0) * side
        return remote(last.at[batch(s)], solved.at[zone, batch(s)], s_last, s_recv.at[zone, s], col=target)

    def solve_last(s):
        value = solve_up(state[batch(s)])
        state[batch(s)] = value
        last[batch(s)] = value.astype(BF16)
        pl.when(zone > 0)(lambda: last_copy(s).start())

        @pl.when(zone > 1)
        def _():
            for d in range(1, side):
                hint_copy(d, s).start()


    def out_copy(m):
        return pltpu.make_async_copy(taken.at[span(m)], out_ref.at[span(m)], out_sem)

    def one_copy(m):
        return remote(send1.at[m], recv1.at[m], one_send.at[m % 2], one_recv.at[m], row=sibling)

    def two_copy(m, d):
        return remote(send2.at[m, d - 1], recv2.at[m, d - 1], two_send.at[m, d - 1], two_recv.at[m, d - 1], row=far[d - 1])

    def first(m, carry):
        send1[m] = dot_t(factors_ref[span(m)], gathered[1 - core]).astype(BF16)
        pl.when(m > start + 1)(lambda: one_copy(m - 2).wait_send())
        one_copy(m).start()
        return carry

    def second(m, carry):
        own1[m] = dot_t(factors_ref[span(m)], gathered[core])
        one_copy(m).wait_recv()
        for d in range(1, chips):
            there = pl.ds(pl.multiple_of(((chip + d) % chips) * width, width), width)

            @pl.when(m < CHUNKS - wants[d])
            def _():
                send2[m, d - 1] = (own1[m, :, there] + recv1[m, :, there].astype(F32)).astype(BF16)
                two_copy(m, d).start()

        pl.when(m + 1 < n_made)(lambda: [first(m + 1, 0)] and None)
        return carry

    def third(m, carry):
        here = pl.ds(pl.multiple_of(chip * width, width), width)
        total = own1[m, :, here] + recv1[m, :, here].astype(F32)
        for d in range(1, chips):
            two_copy(m, d).wait_recv()
            total = total + recv2[m, d - 1].astype(F32)
        taken[span(m)] = rhs_ref[span(m)] - total
        out_copy(m).start()
        return carry

    def finish(m, carry):
        pl.when(m > n_made - 3)(lambda: one_copy(m).wait_send())
        for d in range(1, chips):
            pl.when(m < CHUNKS - wants[d])(lambda: two_copy(m, d).wait_send())
        return carry

    n_swap = CHUNKS - n_extra
    fewest = wants[0]
    for d in range(1, chips):
        fewest = jnp.minimum(fewest, wants[d])
    n_made = CHUNKS - fewest
    start = jnp.where(owner, block // step_rows, 0)

    def extra_hand_on(g, carry):
        for d in range(1, chips):
            extra_arriving(g, d).wait_recv()
            extra_forward(g, d).start()
        return carry

    def far_of(d):
        return ((chip + d) % chips) * 2 + core

    def extra_product(g, carry):
        rows = span(CHUNKS - 1 - g)
        total = jnp.zeros((step_rows, width), F32)
        theirs = extra.at[g, 1 - core]
        for d in range(n_row):
            source = far_of(d) if d < chips else (far_of(d - chips) // 2) * 2 + 1 - core
            part_of = solved[source // pieces, :, pl.ds(pl.multiple_of((source % pieces) * cols, cols), cols)]
            if d == 0:
                total = total + dot_t(factors_ref[rows], part_of)
            else:
                if d == chips:
                    remote(theirs, theirs, x_fwd.at[g, 0], x_recv.at[g, chips - 1], row=sibling).wait_recv()
                total = total + dot_t(extra[g, source % 2, source // 2], part_of)
        taken[rows] = rhs_ref[rows] - total
        out_copy(CHUNKS - 1 - g).start()
        return carry

    def extra_finish(g, carry):
        for d in range(chips):
            pl.when(g < wants[d])(lambda: extra_copy(g, d).wait_send())

        @pl.when(g < n_extra)
        def _():
            for d in range(1, chips):
                extra_forward(g, d).wait_send()

        return carry

    def loaded():
        factors_copy.wait()
        rhs_copy.wait()

    def first_products():
        def arrive(s, carry):
            local_copy(0, s, 0).wait()
            for d in range(1, n_row):
                source = (row + d) % n_row
                piece = gathered.at[source % 2, batch(s, (source // 2) * width)]
                taken_on = jnp.logical_and(lender, source // 2 != chip)
                arrived = remote(piece, piece, g_local.at[s], g_recv.at[source, s], row=source)
                pl.when(jnp.logical_not(taken_on))(arrived.wait_recv)
            return carry

        lax.fori_loop(0, SUBS, arrive, 0)
        first(start, 0)

    def batches(what):
        def one(s, carry):
            what(s)
            return carry

        lax.fori_loop(0, SUBS, one, 0)

    def prepare():
        diag_copy.wait()
        work_copy.wait()
        down = lax.broadcasted_iota(jnp.int32, (block, block), 0)
        across = lax.broadcasted_iota(jnp.int32, (block, block), 1)
        matrix = diag[...]
        low[...] = jnp.where(down > across, matrix, 0.0).astype(BF16)
        up[...] = jnp.where(down < across, matrix, 0.0).astype(BF16)
        scale[...] = jnp.sum(jnp.where(down == across, matrix, 0.0), axis=0, keepdims=True)
        state[...] = work[...].T

    def products():
        first_products()
        lax.fori_loop(start, n_made, second, 0)

    final = slot(steps - 1) * pieces // 2
    sooner = jnp.logical_and(jnp.logical_not(owner), jnp.logical_and(zone == 0, final != chip))
    opens = jnp.logical_and(owner, zone == 0)

    @pl.when(opens)
    def _():
        prepare()
        batches(lambda s: solve_first(s, False))

    pl.semaphore_wait(barrier, n_row - 1 + jnp.where(owner, ends + side - 1, 1 + jnp.where(helper, beyond, 0)))
    @pl.when(sends_panel)
    def _():
        for mine in (False, True):
            for c in range(CUTS):
                near_copy(mine, c).start()

    @pl.when(owner)
    def _():
        panel_own.wait()
        pl.when(leading == row)(lambda: far_sends(leading))

    pl.when(opens)(lambda: batches(lambda s: pass_on(zone, zone, s)))
    lax.fori_loop(0, jnp.where(owner, 0, head), extra_start, 0)
    pl.when(jnp.logical_and(owner, zone > 0))(prepare)
    factors_copy.start()
    rhs_copy.start()

    @pl.when(owner)
    def _():

        pl.when(leading != row)(lambda: far_sends(leading))
        far_sends(trailing)
        lax.fori_loop(0, jnp.where(zone == 0, head, 0), extra_start, 0)
        pl.when(zone == 0)(relay_back)

        def hop(i, carry):
            t = jnp.where(i < zone, i, i + 1)
            j = slot(t)

            late = jnp.logical_and(is_far(j * pieces), i < zone)

            def take(s):
                arrival(j, s).wait_recv()
                pass_on(t, j, s)

            @pl.when(late)
            def _():
                batches(take)
                relay_panel(j)

            def one(s):
                pl.when(jnp.logical_not(late))(lambda: take(s))
                pl.when(s == 0)(lambda: arrive_panel(j))
                update(j, s)
                pl.when(i + 1 == zone)(lambda: solve_first(s))
                pl.when(jnp.logical_and(i == steps - 2, zone > 0))(lambda: solve_last(s))

            batches(one)
            lax.fori_loop(0, jnp.where(jnp.logical_and(waits, i == 0), head, 0), extra_start, 0)
            lax.fori_loop(head, jnp.where(i == 1, GATHER, head), extra_start, 0)
            pl.when(i + 1 == zone)(relay_back)
            pl.when(jnp.logical_and(lender, i == jnp.maximum(my_turn - 1, 0)))(lambda: batches(lend))
            return carry

        lax.fori_loop(0, steps - 1, hop, 0)

        pl.when(zone > 1)(lambda: batches(lambda s: skip_last(s).start()))

        @pl.when(put_off)
        def _():
            for t in range(steps - 1):
                batches(lambda s: sides(t, t, s))

    @pl.when(jnp.logical_not(owner))
    def _():
        loaded()

        def hop(i, carry):
            t = jnp.where(put_off, (i + steps - 1) % steps, i)
            j = slot(t)

            def one(s):
                arrival(j, s).wait_recv()
                pass_on(t, j, s)

                @pl.when(jnp.logical_and(t == steps - 1, zone > 1))
                def _():
                    hint_copy(1, s).wait_recv()
                    backwards(s)

            batches(one)
            lax.fori_loop(head, jnp.where(i == 2, GATHER, head), extra_start, 0)
            return carry

        def each(i, carry):
            pl.when(jnp.logical_and(sooner, i == steps - 1))(products)
            return hop(i, carry)

        lax.fori_loop(0, steps, each, 0)

    pl.when(owner)(loaded)
    done = jnp.where(jnp.logical_and(zone == 0, jnp.logical_not(jnp.logical_or(owner, sooner))), jnp.minimum(n_extra, AHEAD), 0)
    lax.fori_loop(0, done, extra_hand_on, 0)
    lax.fori_loop(0, done, extra_product, 0)
    pl.when(jnp.logical_not(sooner))(products)
    lax.fori_loop(done, n_extra, extra_hand_on, 0)
    pl.when(jnp.logical_and(owner, zone == 0))(lambda: batches(solve_last))
    lax.fori_loop(done, n_extra, extra_product, 0)

    @pl.when(owner)
    def _():
        taken[pl.ds(0, block)] = state[...].T
        for m in range(block // step_rows):
            out_copy(m).start()

    lax.fori_loop(start, n_swap, third, 0)
    lax.fori_loop(start, n_made, finish, 0)
    lax.fori_loop(0, GATHER, extra_finish, 0)

    @pl.when(sends_panel)
    def _():
        sent(panel.at[row], f_send)

    for source in (pair, pair + 1):
        @pl.when(needed(source))
        def _():
            for d in range(1, chips):
                sent(half_block(source, core), f_far.at[source % 2, d - 1])

    def drain(t, carry):
        j = slot(t)

        for p in range(pieces):
            source = j * pieces + p

            @pl.when(jnp.logical_and(is_far(source), t != zone))
            def _():
                sent(half_block(source, core), f_fwd.at[source])

        pl.when(chains(t))(lambda: sent(solved.at[t], s_chain.at[jnp.where(t == 0, 0, 1)]))

        @pl.when(t == zone)
        def _():
            for z in range(2, steps):
                pl.when(helps(z))(lambda: sent(solved.at[zone], s_help.at[z]))

        @pl.when(has_sides(j))
        def _():
            for d in range(1, side):
                sent(solved.at[j], s_side.at[t, d - 1])

        for p in range(pieces):
            pl.when(shares_with(t, j, p))(lambda: sent(gathered.at[0, pl.ds(0, width)], s_row.at[t, p]))

        return carry

    lax.fori_loop(0, steps, drain, 0)

    pltpu.make_async_copy(taken, out_ref, out_sem).wait()

    @pl.when(lender)
    def _():
        for d in range(1, side):
            for k in range(2 * (chips - 1)):
                sent(gathered.at[0, pl.ds(0, width)], s_lend.at[d - 1, k])

    pl.when(jnp.logical_and(owner, zone > 0))(lambda: sent(last, s_last))

    @pl.when(jnp.logical_and(owner, zone > 1))
    def _():
        sent(last, s_chain.at[2])
        for d in range(1, side):
            sent(last, s_hint.at[d - 1])

    @pl.when(jnp.logical_and(jnp.logical_not(owner), zone > 1))
    def _():
        sent(last, s_chain.at[0])
        for z in range(steps - 3):
            pl.when(helps_back(z))(lambda: sent(last, s_help.at[z]))


def body(rhs, factors, diag_inv):
    n_row, n_col = lax.axis_size("row"), lax.axis_size("col")
    rows_dev, width = rhs.shape
    cols = factors.shape[1]
    steps, block = diag_inv.shape[:2]
    pieces, chips, side = block // cols, n_row // 2, n_col // steps
    step_rows = rows_dev // CHUNKS
    dma = pltpu.SemaphoreType.DMA
    taken = pl.pallas_call(
        functools.partial(kernel, n_row, n_col, steps, block),
        out_shape=jax.ShapeDtypeStruct(rhs.shape, F32),
        in_specs=[pl.BlockSpec(memory_space=pl.ANY)] * 3,
        out_specs=pl.BlockSpec(memory_space=pl.ANY),
        scratch_shapes=[
            pltpu.VMEM(rhs.shape, F32),
            pltpu.VMEM(factors.shape, BF16),
            pltpu.VMEM((GATHER, 2, chips, step_rows, cols), BF16),
            pltpu.VMEM(rhs.shape, F32),
            pltpu.VMEM((block, block), F32),
            pltpu.VMEM((block, block), BF16),
            pltpu.VMEM((block, block), BF16),
            pltpu.VMEM((1, block), F32),
            pltpu.VMEM((n_row, block, cols), BF16),
            pltpu.VMEM((steps, width, block), BF16),
            pltpu.VMEM((width, block), BF16),
            pltpu.VMEM((block, width), F32),
            pltpu.VMEM((width, block), F32),
            pltpu.VMEM((2, chips * width, cols), BF16),
            pltpu.VMEM((CHUNKS, step_rows, chips * width), BF16),
            pltpu.VMEM((CHUNKS, step_rows, chips * width), BF16),
            pltpu.VMEM((CHUNKS, step_rows, chips * width), F32),
            pltpu.VMEM((CHUNKS, chips - 1, step_rows, width), BF16),
            pltpu.VMEM((CHUNKS, chips - 1, step_rows, width), BF16),
            dma, dma, dma((2, chips - 1)), dma((n_row, CUTS + 1)), dma((n_row,)),
            dma((3,)), dma((steps, side - 1)), dma((steps, pieces)), dma((side - 1, 2 * (chips - 1))),
            dma((steps,)), dma((side - 1,)), dma((steps, SUBS)), dma((SUBS,)), dma,
            dma((SUBS,)), dma((n_row, SUBS)),
            dma((2,)), dma((CHUNKS,)), dma((CHUNKS, chips - 1)), dma((CHUNKS, chips - 1)),
            dma((GATHER, chips)), dma((GATHER, chips)), dma((GATHER, chips - 1)), dma((4,)), dma,
        ],
        compiler_params=pltpu.CompilerParams(
            collective_id=0, has_side_effects=True, vmem_limit_bytes=50 * 1024 * 1024
        ),
    )(rhs, factors, diag_inv)
    return taken


def solution(mesh):
    placed = (P("col", "row"), P("col", "row"), P())
    return jax.shard_map(
        body, mesh=mesh, in_specs=placed, out_specs=P("col", "row"), check_vma=False
    )
```

```python
import functools

import jax
import jax.numpy as jnp
from jax import lax
from jax.experimental import pallas as pl
from jax.experimental.pallas import tpu as pltpu
from jax.sharding import PartitionSpec as P

MESH = pl.DeviceIdType.MESH
F32 = jnp.float32
BF16 = jnp.bfloat16
CHUNKS = 8
SUBS = 2
CUTS = 2
GATHER = 4
NEAR0, FAR0, NEAR1, FAR1, REST1 = 2, 3, 4, 4, 2
HEAD0, HEAD1 = 2, 4
AHEAD = 3


def remote(src, dst, send_sem, recv_sem, **device):
    return pltpu.make_async_remote_copy(
        src_ref=src,
        dst_ref=dst,
        send_sem=send_sem,
        recv_sem=recv_sem,
        device_id=device,
        device_id_type=MESH,
    )


def dot(a, b):
    return jnp.dot(a, b, preferred_element_type=F32)


def dot_t(a, b):
    return lax.dot_general(a, b, (((1,), (1,)), ((), ())), preferred_element_type=F32)


def split(value):
    high = value.astype(BF16)
    return high, (value - high.astype(F32)).astype(BF16)


def kernel(
    n_row, n_col, steps, block,
    rhs_hbm, factors_hbm, diag_ref, out_ref,
    rhs_ref, factors_ref, extra, taken,
    diag, low_hi, low_lo, up_hi, up_lo, panel, solved, last, work, state, gathered,
    send1, recv1, own1, send2, recv2,
    diag_sem, f_send, f_far, f_recv, f_fwd, s_chain, s_side, s_row, s_lend, s_help, s_hint, s_recv, l_recv, s_last, g_local, g_recv,
    one_send, one_recv, two_send, two_recv, x_send, x_recv, x_fwd, load_sem, out_sem,
):
    rows_dev, width = rhs_hbm.shape
    cols = factors_ref.shape[1]
    pieces = block // cols
    chips = n_row // 2
    side = n_col // steps
    row = lax.axis_index("row")
    col = lax.axis_index("col")
    chip, core = row // 2, row % 2
    sibling = chip * 2 + 1 - core
    zone, lane = col // side, col % side
    owner = lane == 0
    helper = lane == 1
    base = zone * side

    diag_copy = pltpu.make_async_copy(diag_ref.at[zone], diag, diag_sem)
    rhs_copy = pltpu.make_async_copy(rhs_hbm, rhs_ref, load_sem.at[0])
    factors_copy = pltpu.make_async_copy(factors_hbm, factors_ref, load_sem.at[1])
    work_copy = pltpu.make_async_copy(rhs_hbm.at[pl.ds(0, block)], work, load_sem.at[2])
    panel_own = pltpu.make_async_copy(factors_hbm.at[pl.ds(0, block)], panel.at[row], load_sem.at[3])
    @pl.when(owner)
    def _():
        diag_copy.start()
        work_copy.start()
        panel_own.start()


    barrier = pltpu.get_barrier_semaphore()
    for d in range(1, n_row):
        pl.semaphore_signal(barrier, inc=1, device_id={"row": (row + d) % n_row}, device_id_type=MESH)

    def greet(other):
        pl.semaphore_signal(barrier, inc=1, device_id={"col": other}, device_id_type=MESH)

    @pl.when(owner)
    def _():
        for d in range(1, side):
            greet(base + d)

    pl.when(jnp.logical_and(owner, zone > 0))(lambda: greet(base - side))
    pl.when(jnp.logical_and(owner, zone < steps - 1))(lambda: greet(base + side))
    pl.when(jnp.logical_not(owner))(lambda: greet(base))
    for z in range(1, steps - 2):
        pl.when(jnp.logical_and(owner, zone > z + 1))(lambda: greet(z * side + 1))
    beyond = jnp.where(jnp.logical_and(zone > 0, zone < steps - 2), steps - 2 - zone, 0)
    ends = jnp.where(zone > 0, 1, 0) + jnp.where(zone < steps - 1, 1, 0)

    far = [((chip + d) % chips) * 2 + core for d in range(1, chips)]
    sends_panel = jnp.logical_and(owner, row // pieces != zone)
    half = block // 2
    cut_rows = half // CUTS
    pair = chip * 2
    later = pair // pieces > zone
    leading = jnp.where(later, pair + 1, pair)
    trailing = jnp.where(later, pair, pair + 1)

    def cut(h, c):
        return pl.ds(pl.multiple_of(h * half + c * cut_rows, cut_rows), cut_rows)

    def needed(source):
        return jnp.logical_and(owner, source // pieces != zone)

    def near_copy(mine, c):
        rows = cut(core if mine else 1 - core, c)
        there = f_recv.at[row, CUTS if mine else c]
        return remote(factors_hbm.at[rows], panel.at[row, rows], f_send, there, row=sibling)

    def far_copy(source, d, c):
        piece = panel.at[source, cut(core, c)]
        return remote(piece, piece, f_far.at[source % 2, d - 1], f_recv.at[source, c], row=far[d - 1])

    def arriving(source, c):
        piece = panel.at[source, cut(core, c)]
        return remote(piece, piece, f_fwd.at[source], f_recv.at[source, c], row=sibling)

    def relay_copy(source, c):
        piece = panel.at[source, cut(core, c)]
        return remote(piece, piece, f_fwd.at[source], f_recv.at[source, CUTS], row=sibling)

    def half_block(source, h):
        return panel.at[source, pl.ds(pl.multiple_of(h * half, half), half)]

    def far_sends(source):
        @pl.when(needed(source))
        def _():
            @pl.when(source != row)
            def _():
                for c in range(CUTS):
                    arriving(source, c).wait_recv()

            for d in range(1, chips):
                for c in range(CUTS):
                    far_copy(source, d, c).start()


    step_rows = rows_dev // CHUNKS

    def want(c):
        first_zone = jnp.where(owner, jnp.where(c * 2 < chips, NEAR0, FAR0), jnp.where(c * 2 < chips, NEAR1, FAR1))
        return jnp.where(zone == 0, first_zone, jnp.where(owner, jnp.where(zone < steps - 1, 1, 0), REST1))

    n_extra = want(chip)
    wants = [want((chip + d) % chips) for d in range(chips)]
    head = jnp.where(owner, HEAD0, HEAD1)

    def span(m):
        return pl.ds(pl.multiple_of(m * step_rows, step_rows), step_rows)

    def extra_copy(g, d):
        return remote(
            factors_hbm.at[span(CHUNKS - 1 - g)], extra.at[g, core, chip], x_send.at[g, d], x_recv.at[g, (chips - 1 if d == 0 else chips - 1 - d)],
            row=far[d - 1] if d else sibling,
        )

    def extra_arriving(g, d):
        piece = extra.at[g, core, far[d - 1] // 2]
        return remote(piece, piece, x_fwd.at[g, d - 1], x_recv.at[g, d - 1], row=sibling)

    def extra_forward(g, d):
        piece = extra.at[g, core, far[d - 1] // 2]
        return remote(piece, piece, x_fwd.at[g, d - 1], x_recv.at[g, chips - 1], row=sibling)

    def extra_start(g, carry):
        for d in range(chips):
            pl.when(g < wants[d])(lambda: extra_copy(g, d).start())
        return carry

    waits = jnp.logical_and(owner, zone > 0)
    sub = width // SUBS

    def batch(s, start=0):
        return pl.ds(pl.multiple_of(start + s * sub, sub), sub)

    def stacked(value):
        high, low = split(value)
        return high, jnp.concatenate([high, low])

    def folded(both, more):
        return both[:sub] + (both[sub:] + more)

    def solve_low(value):
        high, both = stacked(value)
        top = folded(dot_t(both[:, :half], low_hi[:half, :half]), dot_t(high[:, :half], low_lo[:half, :half]))
        return jnp.concatenate([top, folded(dot_t(both, low_hi[half:]), dot_t(high, low_lo[half:]))], axis=1)

    def solve_up(value):
        high, both = stacked(value)
        end = folded(dot_t(both[:, half:], up_hi[half:, half:]), dot_t(high[:, half:], up_lo[half:, half:]))
        return jnp.concatenate([folded(dot_t(both, up_hi[:half]), dot_t(high, up_lo[:half])), end], axis=1)

    def slot(t):
        return jnp.where(t <= zone, t, steps + zone - t)

    def is_far(source):
        return jnp.logical_and(owner, source // 2 != chip)

    def relay_panel(j):
        for p in range(pieces):
            source = j * pieces + p

            @pl.when(is_far(source))
            def _():
                for c in range(CUTS):
                    arriving(source, c).wait_recv()
                    relay_copy(source, c).start()

    def relay_back():
        def one(i, carry):
            relay_panel(steps - 1 - i)
            return carry

        lax.fori_loop(0, steps - 1 - zone, one, 0)

    def arrive_panel(j):
        for p in range(pieces):
            source = j * pieces + p

            @pl.when(source != row)
            def _():
                piece = half_block(source, 1 - core)
                remote(piece, piece, f_fwd.at[source], f_recv.at[source, CUTS], row=sibling).wait_recv()

    def chain_copy(t, s):
        piece = solved.at[t, batch(s)]
        k = jnp.where(t == 0, 0, 1)
        return remote(
            piece, piece, s_chain.at[k], s_recv.at[t, s], col=jnp.minimum(zone + 1, steps - 1) * side
        )

    def chains(t):
        return jnp.logical_and(owner, jnp.logical_and((t == 0) | (t == zone), zone < steps - 1))

    def arrival(j, s):
        piece = solved.at[j, batch(s)]
        return remote(piece, piece, s_chain.at[0], s_recv.at[j, s], col=col)

    def help_copy(z, s):
        piece = solved.at[zone, batch(s)]
        return remote(piece, piece, s_help.at[z], s_recv.at[zone, s], col=z * side)

    def help_last(z, s):
        return remote(last.at[batch(s)], solved.at[zone, batch(s)], s_help.at[z], s_recv.at[zone, s], col=z * side)

    def hint_copy(d, s):
        return remote(last.at[batch(s)], last.at[batch(s)], s_hint.at[d - 1], l_recv.at[s], col=base + d)

    def lane_last(s):
        return remote(last.at[batch(s)], solved.at[zone, batch(s)], s_chain.at[0], s_recv.at[zone, s], col=lane)

    def skip_last(s):
        target = jnp.maximum(zone - 2, 0) * side
        return remote(last.at[batch(s)], solved.at[zone, batch(s)], s_chain.at[2], s_recv.at[zone, s], col=target)

    def helps(z):
        return jnp.logical_and(helper, jnp.logical_and(z > zone + 1, zone > 0))

    def helps_back(z):
        return jnp.logical_and(helper, z < zone - 2)

    def forwards(s):
        for z in range(2, steps):
            pl.when(helps(z))(lambda: help_copy(z, s).start())

    def backwards(s):
        for z in reversed(range(steps - 3)):
            pl.when(helps_back(z))(lambda: help_last(z, s).start())
        lane_last(s).start()

    def side_copy(t, j, d, s):
        piece = solved.at[j, batch(s)]
        return remote(piece, piece, s_side.at[t, d - 1], s_recv.at[j, s], col=base + d)

    def lends(t):
        return jnp.logical_and(zone == 0, t < steps)

    def row_copy(t, j, s, p):
        return remote(
            solved.at[j, batch(s), pl.ds(p * cols, cols)], gathered.at[core, batch(s, chip * width)],
            s_row.at[t, p], g_recv.at[row, s], row=j * pieces + p,
        )

    def local_copy(j, s, p):
        return pltpu.make_async_copy(
            solved.at[j, batch(s), pl.ds(p * cols, cols)], gathered.at[core, batch(s, chip * width)], g_local.at[s]
        )

    def shares_with(t, j, p):
        target = j * pieces + p
        lent = jnp.logical_and(lends(t), target // 2 != chip)
        return jnp.logical_and(target != row, jnp.logical_or(owner, jnp.logical_not(lent)))

    my_turn = jnp.where(row // pieces == 0, 0, steps - row // pieces)
    lender = jnp.logical_and(owner, lends(my_turn))

    def lend_copy(d, k, s):
        source = far[k // 2] // 2 * 2 + k % 2
        piece = gathered.at[k % 2, batch(s, (source // 2) * width)]
        return remote(piece, piece, s_lend.at[d - 1, k], g_recv.at[source, s], col=base + d)

    def lend(s):
        for k in range(2 * (chips - 1)):
            lend_copy(1, k, s).wait_recv()
            for d in range(1, side):
                lend_copy(d, k, s).start()

    put_off = zone == steps - 1

    def has_sides(j):
        return jnp.logical_and(owner, jnp.logical_or(zone > 0, j < 2))

    def sent(piece, sem):
        remote(piece, piece, sem, sem, col=col).wait_send()

    def sides(t, j, s):
        for d in range(1, side):
            side_copy(t, j, d, s).start()

    def pass_on(t, j, s):
        pl.when(chains(t))(lambda: chain_copy(t, s).start())

        @pl.when(jnp.logical_and(has_sides(j), jnp.logical_not(jnp.logical_and(put_off, t < zone))))
        def _():
            sides(t, j, s)

        pl.when(t == zone)(lambda: forwards(s))
        for p in range(pieces):
            pl.when(shares_with(t, j, p))(lambda: row_copy(t, j, s, p).start())
            pl.when(j * pieces + p == row)(lambda: local_copy(j, s, p).start())

    def update(j, s):
        total = state[batch(s)]
        for p in range(pieces):
            total = total - dot_t(solved[j, batch(s), pl.ds(p * cols, cols)], panel[j * pieces + p])
        state[batch(s)] = total

    def solve_first(s, sends=True):
        value = state[batch(s)]
        value = value + solve_low(value)
        state[batch(s)] = value
        solved[zone, batch(s)] = value.astype(BF16)
        if sends:
            pass_on(zone, zone, s)

    def last_copy(s):
        target = jnp.where(zone > 0, zone - 1, 0) * side
        return remote(last.at[batch(s)], solved.at[zone, batch(s)], s_last, s_recv.at[zone, s], col=target)

    def solve_last(s):
        value = solve_up(state[batch(s)])
        state[batch(s)] = value
        last[batch(s)] = value.astype(BF16)
        pl.when(zone > 0)(lambda: last_copy(s).start())

        @pl.when(zone > 1)
        def _():
            for d in range(1, side):
                hint_copy(d, s).start()


    def out_copy(m):
        return pltpu.make_async_copy(taken.at[span(m)], out_ref.at[span(m)], out_sem)

    def one_copy(m):
        return remote(send1.at[m], recv1.at[m], one_send.at[m % 2], one_recv.at[m], row=sibling)

    def two_copy(m, d):
        return remote(send2.at[m, d - 1], recv2.at[m, d - 1], two_send.at[m, d - 1], two_recv.at[m, d - 1], row=far[d - 1])

    def first(m, carry):
        send1[m] = dot_t(factors_ref[span(m)], gathered[1 - core]).astype(BF16)
        pl.when(m > start + 1)(lambda: one_copy(m - 2).wait_send())
        one_copy(m).start()
        return carry

    def second(m, carry):
        own1[m] = dot_t(factors_ref[span(m)], gathered[core])
        one_copy(m).wait_recv()
        for d in range(1, chips):
            there = pl.ds(pl.multiple_of(((chip + d) % chips) * width, width), width)

            @pl.when(m < CHUNKS - wants[d])
            def _():
                send2[m, d - 1] = (own1[m, :, there] + recv1[m, :, there].astype(F32)).astype(BF16)
                two_copy(m, d).start()

        pl.when(m + 1 < n_made)(lambda: [first(m + 1, 0)] and None)
        return carry

    def third(m, carry):
        here = pl.ds(pl.multiple_of(chip * width, width), width)
        total = own1[m, :, here] + recv1[m, :, here].astype(F32)
        for d in range(1, chips):
            two_copy(m, d).wait_recv()
            total = total + recv2[m, d - 1].astype(F32)
        taken[span(m)] = rhs_ref[span(m)] - total
        out_copy(m).start()
        return carry

    def finish(m, carry):
        pl.when(m > n_made - 3)(lambda: one_copy(m).wait_send())
        for d in range(1, chips):
            pl.when(m < CHUNKS - wants[d])(lambda: two_copy(m, d).wait_send())
        return carry

    n_swap = CHUNKS - n_extra
    fewest = wants[0]
    for d in range(1, chips):
        fewest = jnp.minimum(fewest, wants[d])
    n_made = CHUNKS - fewest
    start = jnp.where(owner, block // step_rows, 0)

    def extra_hand_on(g, carry):
        for d in range(1, chips):
            extra_arriving(g, d).wait_recv()
            extra_forward(g, d).start()
        return carry

    def far_of(d):
        return ((chip + d) % chips) * 2 + core

    def extra_product(g, carry):
        rows = span(CHUNKS - 1 - g)
        total = jnp.zeros((step_rows, width), F32)
        theirs = extra.at[g, 1 - core]
        for d in range(n_row):
            source = far_of(d) if d < chips else (far_of(d - chips) // 2) * 2 + 1 - core
            part_of = solved[source // pieces, :, pl.ds(pl.multiple_of((source % pieces) * cols, cols), cols)]
            if d == 0:
                total = total + dot_t(factors_ref[rows], part_of)
            else:
                if d == chips:
                    remote(theirs, theirs, x_fwd.at[g, 0], x_recv.at[g, chips - 1], row=sibling).wait_recv()
                total = total + dot_t(extra[g, source % 2, source // 2], part_of)
        taken[rows] = rhs_ref[rows] - total
        out_copy(CHUNKS - 1 - g).start()
        return carry

    def extra_finish(g, carry):
        for d in range(chips):
            pl.when(g < wants[d])(lambda: extra_copy(g, d).wait_send())

        @pl.when(g < n_extra)
        def _():
            for d in range(1, chips):
                extra_forward(g, d).wait_send()

        return carry

    def loaded():
        factors_copy.wait()
        rhs_copy.wait()

    def first_products():
        def arrive(s, carry):
            local_copy(0, s, 0).wait()
            for d in range(1, n_row):
                source = (row + d) % n_row
                piece = gathered.at[source % 2, batch(s, (source // 2) * width)]
                taken_on = jnp.logical_and(lender, source // 2 != chip)
                arrived = remote(piece, piece, g_local.at[s], g_recv.at[source, s], row=source)
                pl.when(jnp.logical_not(taken_on))(arrived.wait_recv)
            return carry

        lax.fori_loop(0, SUBS, arrive, 0)
        first(start, 0)

    def batches(what):
        def one(s, carry):
            what(s)
            return carry

        lax.fori_loop(0, SUBS, one, 0)

    def prepare():
        diag_copy.wait()
        work_copy.wait()
        down = lax.broadcasted_iota(jnp.int32, (block, block), 0)
        across = lax.broadcasted_iota(jnp.int32, (block, block), 1)
        matrix = diag[...]
        low_hi[...], low_lo[...] = split(jnp.where(down > across, matrix, 0.0))
        up_hi[...], up_lo[...] = split(jnp.where(down <= across, matrix, 0.0))
        state[...] = work[...].T

    def products():
        first_products()
        lax.fori_loop(start, n_made, second, 0)

    final = slot(steps - 1) * pieces // 2
    sooner = jnp.logical_and(jnp.logical_not(owner), jnp.logical_and(zone == 0, final != chip))
    opens = jnp.logical_and(owner, zone == 0)

    @pl.when(opens)
    def _():
        prepare()
        batches(lambda s: solve_first(s, False))

    pl.semaphore_wait(barrier, n_row - 1 + jnp.where(owner, ends + side - 1, 1 + jnp.where(helper, beyond, 0)))
    @pl.when(sends_panel)
    def _():
        for mine in (False, True):
            for c in range(CUTS):
                near_copy(mine, c).start()

    @pl.when(owner)
    def _():
        panel_own.wait()
        pl.when(leading == row)(lambda: far_sends(leading))

    pl.when(opens)(lambda: batches(lambda s: pass_on(zone, zone, s)))
    lax.fori_loop(0, jnp.where(owner, 0, head), extra_start, 0)
    pl.when(jnp.logical_and(owner, zone > 0))(prepare)
    factors_copy.start()
    rhs_copy.start()

    @pl.when(owner)
    def _():

        pl.when(leading != row)(lambda: far_sends(leading))
        far_sends(trailing)
        lax.fori_loop(0, jnp.where(zone == 0, head, 0), extra_start, 0)
        pl.when(zone == 0)(relay_back)

        def hop(i, carry):
            t = jnp.where(i < zone, i, i + 1)
            j = slot(t)

            late = jnp.logical_and(is_far(j * pieces), i < zone)

            def take(s):
                arrival(j, s).wait_recv()
                pass_on(t, j, s)

            @pl.when(late)
            def _():
                batches(take)
                relay_panel(j)

            def one(s):
                pl.when(jnp.logical_not(late))(lambda: take(s))
                pl.when(s == 0)(lambda: arrive_panel(j))
                update(j, s)
                pl.when(i + 1 == zone)(lambda: solve_first(s))
                pl.when(jnp.logical_and(i == steps - 2, zone > 0))(lambda: solve_last(s))

            batches(one)
            lax.fori_loop(0, jnp.where(jnp.logical_and(waits, i == 0), head, 0), extra_start, 0)
            lax.fori_loop(head, jnp.where(i == 1, GATHER, head), extra_start, 0)
            pl.when(i + 1 == zone)(relay_back)
            pl.when(jnp.logical_and(lender, i == jnp.maximum(my_turn - 1, 0)))(lambda: batches(lend))
            return carry

        lax.fori_loop(0, steps - 1, hop, 0)

        pl.when(zone > 1)(lambda: batches(lambda s: skip_last(s).start()))

        @pl.when(put_off)
        def _():
            for t in range(steps - 1):
                batches(lambda s: sides(t, t, s))

    @pl.when(jnp.logical_not(owner))
    def _():
        loaded()

        def hop(i, carry):
            t = jnp.where(put_off, (i + steps - 1) % steps, i)
            j = slot(t)

            def one(s):
                arrival(j, s).wait_recv()
                pass_on(t, j, s)

                @pl.when(jnp.logical_and(t == steps - 1, zone > 1))
                def _():
                    hint_copy(1, s).wait_recv()
                    backwards(s)

            batches(one)
            lax.fori_loop(head, jnp.where(i == 2, GATHER, head), extra_start, 0)
            return carry

        def each(i, carry):
            pl.when(jnp.logical_and(sooner, i == steps - 1))(products)
            return hop(i, carry)

        lax.fori_loop(0, steps, each, 0)

    pl.when(owner)(loaded)
    done = jnp.where(jnp.logical_and(zone == 0, jnp.logical_not(jnp.logical_or(owner, sooner))), jnp.minimum(n_extra, AHEAD), 0)
    lax.fori_loop(0, done, extra_hand_on, 0)
    lax.fori_loop(0, done, extra_product, 0)
    pl.when(jnp.logical_not(sooner))(products)
    lax.fori_loop(done, n_extra, extra_hand_on, 0)
    pl.when(jnp.logical_and(owner, zone == 0))(lambda: batches(solve_last))
    lax.fori_loop(done, n_extra, extra_product, 0)

    @pl.when(owner)
    def _():
        taken[pl.ds(0, block)] = state[...].T
        for m in range(block // step_rows):
            out_copy(m).start()

    lax.fori_loop(start, n_swap, third, 0)
    lax.fori_loop(start, n_made, finish, 0)
    lax.fori_loop(0, GATHER, extra_finish, 0)

    @pl.when(sends_panel)
    def _():
        sent(panel.at[row], f_send)

    for source in (pair, pair + 1):
        @pl.when(needed(source))
        def _():
            for d in range(1, chips):
                sent(half_block(source, core), f_far.at[source % 2, d - 1])

    def drain(t, carry):
        j = slot(t)

        for p in range(pieces):
            source = j * pieces + p

            @pl.when(jnp.logical_and(is_far(source), t != zone))
            def _():
                sent(half_block(source, core), f_fwd.at[source])

        pl.when(chains(t))(lambda: sent(solved.at[t], s_chain.at[jnp.where(t == 0, 0, 1)]))

        @pl.when(t == zone)
        def _():
            for z in range(2, steps):
                pl.when(helps(z))(lambda: sent(solved.at[zone], s_help.at[z]))

        @pl.when(has_sides(j))
        def _():
            for d in range(1, side):
                sent(solved.at[j], s_side.at[t, d - 1])

        for p in range(pieces):
            pl.when(shares_with(t, j, p))(lambda: sent(gathered.at[0, pl.ds(0, width)], s_row.at[t, p]))

        return carry

    lax.fori_loop(0, steps, drain, 0)

    pltpu.make_async_copy(taken, out_ref, out_sem).wait()

    @pl.when(lender)
    def _():
        for d in range(1, side):
            for k in range(2 * (chips - 1)):
                sent(gathered.at[0, pl.ds(0, width)], s_lend.at[d - 1, k])

    pl.when(jnp.logical_and(owner, zone > 0))(lambda: sent(last, s_last))

    @pl.when(jnp.logical_and(owner, zone > 1))
    def _():
        sent(last, s_chain.at[2])
        for d in range(1, side):
            sent(last, s_hint.at[d - 1])

    @pl.when(jnp.logical_and(jnp.logical_not(owner), zone > 1))
    def _():
        sent(last, s_chain.at[0])
        for z in range(steps - 3):
            pl.when(helps_back(z))(lambda: sent(last, s_help.at[z]))


def body(rhs, factors, diag_inv):
    n_row, n_col = lax.axis_size("row"), lax.axis_size("col")
    rows_dev, width = rhs.shape
    cols = factors.shape[1]
    steps, block = diag_inv.shape[:2]
    pieces, chips, side = block // cols, n_row // 2, n_col // steps
    step_rows = rows_dev // CHUNKS
    dma = pltpu.SemaphoreType.DMA
    taken = pl.pallas_call(
        functools.partial(kernel, n_row, n_col, steps, block),
        out_shape=jax.ShapeDtypeStruct(rhs.shape, F32),
        in_specs=[pl.BlockSpec(memory_space=pl.ANY)] * 3,
        out_specs=pl.BlockSpec(memory_space=pl.ANY),
        scratch_shapes=[
            pltpu.VMEM(rhs.shape, F32),
            pltpu.VMEM(factors.shape, BF16),
            pltpu.VMEM((GATHER, 2, chips, step_rows, cols), BF16),
            pltpu.VMEM(rhs.shape, F32),
            pltpu.VMEM((block, block), F32),
            pltpu.VMEM((block, block), BF16),
            pltpu.VMEM((block, block), BF16),
            pltpu.VMEM((block, block), BF16),
            pltpu.VMEM((block, block), BF16),
            pltpu.VMEM((n_row, block, cols), BF16),
            pltpu.VMEM((steps, width, block), BF16),
            pltpu.VMEM((width, block), BF16),
            pltpu.VMEM((block, width), F32),
            pltpu.VMEM((width, block), F32),
            pltpu.VMEM((2, chips * width, cols), BF16),
            pltpu.VMEM((CHUNKS, step_rows, chips * width), BF16),
            pltpu.VMEM((CHUNKS, step_rows, chips * width), BF16),
            pltpu.VMEM((CHUNKS, step_rows, chips * width), F32),
            pltpu.VMEM((CHUNKS, chips - 1, step_rows, width), BF16),
            pltpu.VMEM((CHUNKS, chips - 1, step_rows, width), BF16),
            dma, dma, dma((2, chips - 1)), dma((n_row, CUTS + 1)), dma((n_row,)),
            dma((3,)), dma((steps, side - 1)), dma((steps, pieces)), dma((side - 1, 2 * (chips - 1))),
            dma((steps,)), dma((side - 1,)), dma((steps, SUBS)), dma((SUBS,)), dma,
            dma((SUBS,)), dma((n_row, SUBS)),
            dma((2,)), dma((CHUNKS,)), dma((CHUNKS, chips - 1)), dma((CHUNKS, chips - 1)),
            dma((GATHER, chips)), dma((GATHER, chips)), dma((GATHER, chips - 1)), dma((4,)), dma,
        ],
        compiler_params=pltpu.CompilerParams(
            collective_id=0, has_side_effects=True, vmem_limit_bytes=50 * 1024 * 1024
        ),
    )(rhs, factors, diag_inv)
    return taken


def solution(mesh):
    placed = (P("col", "row"), P("col", "row"), P())
    return jax.shard_map(
        body, mesh=mesh, in_specs=placed, out_specs=P("col", "row"), check_vma=False
    )
```

```python
import functools

import jax
import jax.numpy as jnp
from jax import lax
from jax.experimental import pallas as pl
from jax.experimental.pallas import tpu as pltpu
from jax.sharding import PartitionSpec as P

MESH = pl.DeviceIdType.MESH
F32 = jnp.float32
BF16 = jnp.bfloat16
CHUNKS = 8
SUBS = 2
CUTS = 1
GATHER = 4
NEAR0, FAR0, NEAR1, FAR1, REST1 = 2, 3, 4, 4, 2
HEAD0, HEAD1 = 2, 4
AHEAD = 3


def remote(src, dst, send_sem, recv_sem, **device):
    return pltpu.make_async_remote_copy(
        src_ref=src,
        dst_ref=dst,
        send_sem=send_sem,
        recv_sem=recv_sem,
        device_id=device,
        device_id_type=MESH,
    )


def dot(a, b):
    return jnp.dot(a, b, preferred_element_type=F32)


def dot_t(a, b):
    return lax.dot_general(a, b, (((1,), (1,)), ((), ())), preferred_element_type=F32)


def split(value):
    high = value.astype(BF16)
    return high, (value - high.astype(F32)).astype(BF16)


def kernel(
    n_row, n_col, steps, block,
    rhs_hbm, factors_hbm, diag_ref, out_ref,
    rhs_ref, factors_ref, extra, taken,
    diag, low_hi, low_lo, up_hi, up_lo, panel, solved, last, work, state, gathered,
    send1, recv1, own1, send2, recv2,
    diag_sem, f_send, f_far, f_recv, f_fwd, s_chain, s_side, s_row, s_lend, s_help, s_hint, s_recv, l_recv, s_last, g_local, g_recv,
    one_send, one_recv, two_send, two_recv, x_send, x_recv, x_fwd, load_sem, out_sem,
):
    rows_dev, width = rhs_hbm.shape
    cols = factors_ref.shape[1]
    pieces = block // cols
    chips = n_row // 2
    side = n_col // steps
    row = lax.axis_index("row")
    col = lax.axis_index("col")
    chip, core = row // 2, row % 2
    sibling = chip * 2 + 1 - core
    zone, lane = col // side, col % side
    owner = lane == 0
    helper = lane == 1
    base = zone * side

    diag_copy = pltpu.make_async_copy(diag_ref.at[zone], diag, diag_sem)
    rhs_copy = pltpu.make_async_copy(rhs_hbm, rhs_ref, load_sem.at[0])
    factors_copy = pltpu.make_async_copy(factors_hbm, factors_ref, load_sem.at[1])
    work_copy = pltpu.make_async_copy(rhs_hbm.at[pl.ds(0, block)], work, load_sem.at[2])
    panel_own = pltpu.make_async_copy(factors_hbm.at[pl.ds(0, block)], panel.at[row], load_sem.at[3])
    @pl.when(owner)
    def _():
        diag_copy.start()
        work_copy.start()
        panel_own.start()


    barrier = pltpu.get_barrier_semaphore()
    for d in range(1, n_row):
        pl.semaphore_signal(barrier, inc=1, device_id={"row": (row + d) % n_row}, device_id_type=MESH)

    def greet(other):
        pl.semaphore_signal(barrier, inc=1, device_id={"col": other}, device_id_type=MESH)

    @pl.when(owner)
    def _():
        for d in range(1, side):
            greet(base + d)

    pl.when(jnp.logical_and(owner, zone > 0))(lambda: greet(base - side))
    pl.when(jnp.logical_and(owner, zone < steps - 1))(lambda: greet(base + side))
    pl.when(jnp.logical_not(owner))(lambda: greet(base))
    for z in range(1, steps - 2):
        pl.when(jnp.logical_and(owner, zone > z + 1))(lambda: greet(z * side + 1))
    beyond = jnp.where(jnp.logical_and(zone > 0, zone < steps - 2), steps - 2 - zone, 0)
    ends = jnp.where(zone > 0, 1, 0) + jnp.where(zone < steps - 1, 1, 0)

    far = [((chip + d) % chips) * 2 + core for d in range(1, chips)]
    sends_panel = jnp.logical_and(owner, row // pieces != zone)
    half = block // 2
    cut_rows = half // CUTS
    pair = chip * 2
    later = pair // pieces > zone
    leading = jnp.where(later, pair + 1, pair)
    trailing = jnp.where(later, pair, pair + 1)

    def cut(h, c):
        return pl.ds(pl.multiple_of(h * half + c * cut_rows, cut_rows), cut_rows)

    def needed(source):
        return jnp.logical_and(owner, source // pieces != zone)

    def near_copy(mine, c):
        rows = cut(core if mine else 1 - core, c)
        there = f_recv.at[row, CUTS if mine else c]
        return remote(factors_hbm.at[rows], panel.at[row, rows], f_send, there, row=sibling)

    def far_copy(source, d, c):
        piece = panel.at[source, cut(core, c)]
        return remote(piece, piece, f_far.at[source % 2, d - 1], f_recv.at[source, c], row=far[d - 1])

    def arriving(source, c):
        piece = panel.at[source, cut(core, c)]
        return remote(piece, piece, f_fwd.at[source], f_recv.at[source, c], row=sibling)

    def relay_copy(source, c):
        piece = panel.at[source, cut(core, c)]
        return remote(piece, piece, f_fwd.at[source], f_recv.at[source, CUTS], row=sibling)

    def half_block(source, h):
        return panel.at[source, pl.ds(pl.multiple_of(h * half, half), half)]

    def far_sends(source):
        @pl.when(needed(source))
        def _():
            @pl.when(source != row)
            def _():
                for c in range(CUTS):
                    arriving(source, c).wait_recv()

            for d in range(1, chips):
                for c in range(CUTS):
                    far_copy(source, d, c).start()


    step_rows = rows_dev // CHUNKS

    def want(c):
        first_zone = jnp.where(owner, jnp.where(c * 2 < chips, NEAR0, FAR0), jnp.where(c * 2 < chips, NEAR1, FAR1))
        return jnp.where(zone == 0, first_zone, jnp.where(owner, jnp.where(zone < steps - 1, 1, 0), REST1))

    n_extra = want(chip)
    wants = [want((chip + d) % chips) for d in range(chips)]
    head = jnp.where(owner, HEAD0, HEAD1)

    def span(m):
        return pl.ds(pl.multiple_of(m * step_rows, step_rows), step_rows)

    def extra_copy(g, d):
        return remote(
            factors_hbm.at[span(CHUNKS - 1 - g)], extra.at[g, core, chip], x_send.at[g, d], x_recv.at[g, (chips - 1 if d == 0 else chips - 1 - d)],
            row=far[d - 1] if d else sibling,
        )

    def extra_arriving(g, d):
        piece = extra.at[g, core, far[d - 1] // 2]
        return remote(piece, piece, x_fwd.at[g, d - 1], x_recv.at[g, d - 1], row=sibling)

    def extra_forward(g, d):
        piece = extra.at[g, core, far[d - 1] // 2]
        return remote(piece, piece, x_fwd.at[g, d - 1], x_recv.at[g, chips - 1], row=sibling)

    def extra_start(g, carry):
        for d in range(chips):
            pl.when(g < wants[d])(lambda: extra_copy(g, d).start())
        return carry

    waits = jnp.logical_and(owner, zone > 0)
    sub = width // SUBS

    def batch(s, start=0):
        return pl.ds(pl.multiple_of(start + s * sub, sub), sub)

    def stacked(value):
        high, low = split(value)
        return high, jnp.concatenate([high, low])

    def folded(both, more):
        return both[:sub] + (both[sub:] + more)

    def solve_low(value):
        high, both = stacked(value)
        top = folded(dot_t(both[:, :half], low_hi[:half, :half]), dot_t(high[:, :half], low_lo[:half, :half]))
        return jnp.concatenate([top, folded(dot_t(both, low_hi[half:]), dot_t(high, low_lo[half:]))], axis=1)

    def solve_up(value):
        high, both = stacked(value)
        end = folded(dot_t(both[:, half:], up_hi[half:, half:]), dot_t(high[:, half:], up_lo[half:, half:]))
        return jnp.concatenate([folded(dot_t(both, up_hi[:half]), dot_t(high, up_lo[:half])), end], axis=1)

    def slot(t):
        return jnp.where(t <= zone, t, steps + zone - t)

    def is_far(source):
        return jnp.logical_and(owner, source // 2 != chip)

    def relay_panel(j):
        for p in range(pieces):
            source = j * pieces + p

            @pl.when(is_far(source))
            def _():
                for c in range(CUTS):
                    arriving(source, c).wait_recv()
                    relay_copy(source, c).start()

    def relay_back():
        def one(i, carry):
            relay_panel(steps - 1 - i)
            return carry

        lax.fori_loop(0, steps - 1 - zone, one, 0)

    def arrive_panel(j):
        for p in range(pieces):
            source = j * pieces + p

            @pl.when(source != row)
            def _():
                piece = half_block(source, 1 - core)
                remote(piece, piece, f_fwd.at[source], f_recv.at[source, CUTS], row=sibling).wait_recv()

    def chain_copy(t, s):
        piece = solved.at[t, batch(s)]
        k = jnp.where(t == 0, 0, 1)
        return remote(
            piece, piece, s_chain.at[k], s_recv.at[t, s], col=jnp.minimum(zone + 1, steps - 1) * side
        )

    def chains(t):
        return jnp.logical_and(owner, jnp.logical_and((t == 0) | (t == zone), zone < steps - 1))

    def arrival(j, s):
        piece = solved.at[j, batch(s)]
        return remote(piece, piece, s_chain.at[0], s_recv.at[j, s], col=col)

    def help_copy(z, s):
        piece = solved.at[zone, batch(s)]
        return remote(piece, piece, s_help.at[z], s_recv.at[zone, s], col=z * side)

    def help_last(z, s):
        return remote(last.at[batch(s)], solved.at[zone, batch(s)], s_help.at[z], s_recv.at[zone, s], col=z * side)

    def hint_copy(d, s):
        return remote(last.at[batch(s)], last.at[batch(s)], s_hint.at[d - 1], l_recv.at[s], col=base + d)

    def lane_last(s):
        return remote(last.at[batch(s)], solved.at[zone, batch(s)], s_chain.at[0], s_recv.at[zone, s], col=lane)

    def skip_last(s):
        target = jnp.maximum(zone - 2, 0) * side
        return remote(last.at[batch(s)], solved.at[zone, batch(s)], s_chain.at[2], s_recv.at[zone, s], col=target)

    def helps(z):
        return jnp.logical_and(helper, jnp.logical_and(z > zone + 1, zone > 0))

    def helps_back(z):
        return jnp.logical_and(helper, z < zone - 2)

    def forwards(s):
        for z in range(2, steps):
            pl.when(helps(z))(lambda: help_copy(z, s).start())

    def backwards(s):
        for z in reversed(range(steps - 3)):
            pl.when(helps_back(z))(lambda: help_last(z, s).start())
        lane_last(s).start()

    def side_copy(t, j, d, s):
        piece = solved.at[j, batch(s)]
        return remote(piece, piece, s_side.at[t, d - 1], s_recv.at[j, s], col=base + d)

    def lends(t):
        return jnp.logical_and(zone == 0, t < steps)

    def row_copy(t, j, s, p):
        return remote(
            solved.at[j, batch(s), pl.ds(p * cols, cols)], gathered.at[core, batch(s, chip * width)],
            s_row.at[t, p], g_recv.at[row, s], row=j * pieces + p,
        )

    def local_copy(j, s, p):
        return pltpu.make_async_copy(
            solved.at[j, batch(s), pl.ds(p * cols, cols)], gathered.at[core, batch(s, chip * width)], g_local.at[s]
        )

    def shares_with(t, j, p):
        target = j * pieces + p
        lent = jnp.logical_and(lends(t), target // 2 != chip)
        return jnp.logical_and(target != row, jnp.logical_or(owner, jnp.logical_not(lent)))

    my_turn = jnp.where(row // pieces == 0, 0, steps - row // pieces)
    lender = jnp.logical_and(owner, lends(my_turn))

    def lend_copy(d, k, s):
        source = far[k // 2] // 2 * 2 + k % 2
        piece = gathered.at[k % 2, batch(s, (source // 2) * width)]
        return remote(piece, piece, s_lend.at[d - 1, k], g_recv.at[source, s], col=base + d)

    def lend(s):
        for k in range(2 * (chips - 1)):
            lend_copy(1, k, s).wait_recv()
            for d in range(1, side):
                lend_copy(d, k, s).start()

    put_off = zone == steps - 1

    def has_sides(j):
        return jnp.logical_and(owner, jnp.logical_or(zone > 0, j < 2))

    def sent(piece, sem):
        remote(piece, piece, sem, sem, col=col).wait_send()

    def sides(t, j, s):
        for d in range(1, side):
            side_copy(t, j, d, s).start()

    def pass_on(t, j, s):
        pl.when(chains(t))(lambda: chain_copy(t, s).start())

        @pl.when(jnp.logical_and(has_sides(j), jnp.logical_not(jnp.logical_and(put_off, t < zone))))
        def _():
            sides(t, j, s)

        pl.when(t == zone)(lambda: forwards(s))
        for p in range(pieces):
            pl.when(shares_with(t, j, p))(lambda: row_copy(t, j, s, p).start())
            pl.when(j * pieces + p == row)(lambda: local_copy(j, s, p).start())

    def update(j, s):
        total = state[batch(s)]
        for p in range(pieces):
            total = total - dot_t(solved[j, batch(s), pl.ds(p * cols, cols)], panel[j * pieces + p])
        state[batch(s)] = total

    def solve_first(s, sends=True):
        value = state[batch(s)]
        value = value + solve_low(value)
        state[batch(s)] = value
        solved[zone, batch(s)] = value.astype(BF16)
        if sends:
            pass_on(zone, zone, s)

    def last_copy(s):
        target = jnp.where(zone > 0, zone - 1, 0) * side
        return remote(last.at[batch(s)], solved.at[zone, batch(s)], s_last, s_recv.at[zone, s], col=target)

    def solve_last(s):
        value = solve_up(state[batch(s)])
        state[batch(s)] = value
        last[batch(s)] = value.astype(BF16)
        pl.when(zone > 0)(lambda: last_copy(s).start())

        @pl.when(zone > 1)
        def _():
            for d in range(1, side):
                hint_copy(d, s).start()


    def out_copy(m):
        return pltpu.make_async_copy(taken.at[span(m)], out_ref.at[span(m)], out_sem)

    def one_copy(m):
        return remote(send1.at[m], recv1.at[m], one_send.at[m % 2], one_recv.at[m], row=sibling)

    def two_copy(m, d):
        return remote(send2.at[m, d - 1], recv2.at[m, d - 1], two_send.at[m, d - 1], two_recv.at[m, d - 1], row=far[d - 1])

    def first(m, carry):
        send1[m] = dot_t(factors_ref[span(m)], gathered[1 - core]).astype(BF16)
        pl.when(m > start + 1)(lambda: one_copy(m - 2).wait_send())
        one_copy(m).start()
        return carry

    def second(m, carry):
        own1[m] = dot_t(factors_ref[span(m)], gathered[core])
        one_copy(m).wait_recv()
        for d in range(1, chips):
            there = pl.ds(pl.multiple_of(((chip + d) % chips) * width, width), width)

            @pl.when(m < CHUNKS - wants[d])
            def _():
                send2[m, d - 1] = (own1[m, :, there] + recv1[m, :, there].astype(F32)).astype(BF16)
                two_copy(m, d).start()

        pl.when(m + 1 < n_made)(lambda: [first(m + 1, 0)] and None)
        return carry

    def third(m, carry):
        here = pl.ds(pl.multiple_of(chip * width, width), width)
        total = own1[m, :, here] + recv1[m, :, here].astype(F32)
        for d in range(1, chips):
            two_copy(m, d).wait_recv()
            total = total + recv2[m, d - 1].astype(F32)
        taken[span(m)] = rhs_ref[span(m)] - total
        out_copy(m).start()
        return carry

    def finish(m, carry):
        pl.when(m > n_made - 3)(lambda: one_copy(m).wait_send())
        for d in range(1, chips):
            pl.when(m < CHUNKS - wants[d])(lambda: two_copy(m, d).wait_send())
        return carry

    n_swap = CHUNKS - n_extra
    fewest = wants[0]
    for d in range(1, chips):
        fewest = jnp.minimum(fewest, wants[d])
    n_made = CHUNKS - fewest
    start = jnp.where(owner, block // step_rows, 0)

    def extra_hand_on(g, carry):
        for d in range(1, chips):
            extra_arriving(g, d).wait_recv()
            extra_forward(g, d).start()
        return carry

    def far_of(d):
        return ((chip + d) % chips) * 2 + core

    def extra_product(g, carry):
        rows = span(CHUNKS - 1 - g)
        total = jnp.zeros((step_rows, width), F32)
        theirs = extra.at[g, 1 - core]
        for d in range(n_row):
            source = far_of(d) if d < chips else (far_of(d - chips) // 2) * 2 + 1 - core
            part_of = solved[source // pieces, :, pl.ds(pl.multiple_of((source % pieces) * cols, cols), cols)]
            if d == 0:
                total = total + dot_t(factors_ref[rows], part_of)
            else:
                if d == chips:
                    remote(theirs, theirs, x_fwd.at[g, 0], x_recv.at[g, chips - 1], row=sibling).wait_recv()
                total = total + dot_t(extra[g, source % 2, source // 2], part_of)
        taken[rows] = rhs_ref[rows] - total
        out_copy(CHUNKS - 1 - g).start()
        return carry

    def extra_finish(g, carry):
        for d in range(chips):
            pl.when(g < wants[d])(lambda: extra_copy(g, d).wait_send())

        @pl.when(g < n_extra)
        def _():
            for d in range(1, chips):
                extra_forward(g, d).wait_send()

        return carry

    def loaded():
        factors_copy.wait()
        rhs_copy.wait()

    def first_products():
        def arrive(s, carry):
            local_copy(0, s, 0).wait()
            for d in range(1, n_row):
                source = (row + d) % n_row
                piece = gathered.at[source % 2, batch(s, (source // 2) * width)]
                taken_on = jnp.logical_and(lender, source // 2 != chip)
                arrived = remote(piece, piece, g_local.at[s], g_recv.at[source, s], row=source)
                pl.when(jnp.logical_not(taken_on))(arrived.wait_recv)
            return carry

        lax.fori_loop(0, SUBS, arrive, 0)
        first(start, 0)

    def batches(what):
        def one(s, carry):
            what(s)
            return carry

        lax.fori_loop(0, SUBS, one, 0)

    def prepare():
        diag_copy.wait()
        work_copy.wait()
        down = lax.broadcasted_iota(jnp.int32, (block, block), 0)
        across = lax.broadcasted_iota(jnp.int32, (block, block), 1)
        matrix = diag[...]
        low_hi[...], low_lo[...] = split(jnp.where(down > across, matrix, 0.0))
        up_hi[...], up_lo[...] = split(jnp.where(down <= across, matrix, 0.0))
        state[...] = work[...].T

    def products():
        first_products()
        lax.fori_loop(start, n_made, second, 0)

    final = slot(steps - 1) * pieces // 2
    sooner = jnp.logical_and(jnp.logical_not(owner), jnp.logical_and(zone == 0, final != chip))
    opens = jnp.logical_and(owner, zone == 0)

    @pl.when(opens)
    def _():
        prepare()
        batches(lambda s: solve_first(s, False))

    pl.semaphore_wait(barrier, n_row - 1 + jnp.where(owner, ends + side - 1, 1 + jnp.where(helper, beyond, 0)))
    @pl.when(sends_panel)
    def _():
        for mine in (False, True):
            for c in range(CUTS):
                near_copy(mine, c).start()

    @pl.when(owner)
    def _():
        panel_own.wait()
        pl.when(leading == row)(lambda: far_sends(leading))

    pl.when(opens)(lambda: batches(lambda s: pass_on(zone, zone, s)))
    lax.fori_loop(0, jnp.where(owner, 0, head), extra_start, 0)
    pl.when(jnp.logical_and(owner, zone > 0))(prepare)
    factors_copy.start()
    rhs_copy.start()

    @pl.when(owner)
    def _():

        pl.when(leading != row)(lambda: far_sends(leading))
        far_sends(trailing)
        lax.fori_loop(0, jnp.where(zone == 0, head, 0), extra_start, 0)
        pl.when(zone == 0)(relay_back)

        def hop(i, carry):
            t = jnp.where(i < zone, i, i + 1)
            j = slot(t)

            late = jnp.logical_and(is_far(j * pieces), i < zone)

            def take(s):
                arrival(j, s).wait_recv()
                pass_on(t, j, s)

            @pl.when(late)
            def _():
                batches(take)
                relay_panel(j)

            def one(s):
                pl.when(jnp.logical_not(late))(lambda: take(s))
                pl.when(s == 0)(lambda: arrive_panel(j))
                update(j, s)
                pl.when(i + 1 == zone)(lambda: solve_first(s))
                pl.when(jnp.logical_and(i == steps - 2, zone > 0))(lambda: solve_last(s))

            batches(one)
            lax.fori_loop(0, jnp.where(jnp.logical_and(waits, i == 0), head, 0), extra_start, 0)
            lax.fori_loop(head, jnp.where(i == 1, GATHER, head), extra_start, 0)
            pl.when(i + 1 == zone)(relay_back)
            pl.when(jnp.logical_and(lender, i == jnp.maximum(my_turn - 1, 0)))(lambda: batches(lend))
            return carry

        lax.fori_loop(0, steps - 1, hop, 0)

        pl.when(zone > 1)(lambda: batches(lambda s: skip_last(s).start()))

        @pl.when(put_off)
        def _():
            for t in range(steps - 1):
                batches(lambda s: sides(t, t, s))

    @pl.when(jnp.logical_not(owner))
    def _():
        loaded()

        def hop(i, carry):
            t = jnp.where(put_off, (i + steps - 1) % steps, i)
            j = slot(t)

            def one(s):
                arrival(j, s).wait_recv()
                pass_on(t, j, s)

                @pl.when(jnp.logical_and(t == steps - 1, zone > 1))
                def _():
                    hint_copy(1, s).wait_recv()
                    backwards(s)

            batches(one)
            lax.fori_loop(head, jnp.where(i == 2, GATHER, head), extra_start, 0)
            return carry

        def each(i, carry):
            pl.when(jnp.logical_and(sooner, i == steps - 1))(products)
            return hop(i, carry)

        lax.fori_loop(0, steps, each, 0)

    pl.when(owner)(loaded)
    done = jnp.where(jnp.logical_and(zone == 0, jnp.logical_not(jnp.logical_or(owner, sooner))), jnp.minimum(n_extra, AHEAD), 0)
    lax.fori_loop(0, done, extra_hand_on, 0)
    lax.fori_loop(0, done, extra_product, 0)
    pl.when(jnp.logical_not(sooner))(products)
    lax.fori_loop(done, n_extra, extra_hand_on, 0)
    pl.when(jnp.logical_and(owner, zone == 0))(lambda: batches(solve_last))
    lax.fori_loop(done, n_extra, extra_product, 0)

    @pl.when(owner)
    def _():
        taken[pl.ds(0, block)] = state[...].T
        for m in range(block // step_rows):
            out_copy(m).start()

    lax.fori_loop(start, n_swap, third, 0)
    lax.fori_loop(start, n_made, finish, 0)
    lax.fori_loop(0, GATHER, extra_finish, 0)

    @pl.when(sends_panel)
    def _():
        sent(panel.at[row], f_send)

    for source in (pair, pair + 1):
        @pl.when(needed(source))
        def _():
            for d in range(1, chips):
                sent(half_block(source, core), f_far.at[source % 2, d - 1])

    def drain(t, carry):
        j = slot(t)

        for p in range(pieces):
            source = j * pieces + p

            @pl.when(jnp.logical_and(is_far(source), t != zone))
            def _():
                sent(half_block(source, core), f_fwd.at[source])

        pl.when(chains(t))(lambda: sent(solved.at[t], s_chain.at[jnp.where(t == 0, 0, 1)]))

        @pl.when(t == zone)
        def _():
            for z in range(2, steps):
                pl.when(helps(z))(lambda: sent(solved.at[zone], s_help.at[z]))

        @pl.when(has_sides(j))
        def _():
            for d in range(1, side):
                sent(solved.at[j], s_side.at[t, d - 1])

        for p in range(pieces):
            pl.when(shares_with(t, j, p))(lambda: sent(gathered.at[0, pl.ds(0, width)], s_row.at[t, p]))

        return carry

    lax.fori_loop(0, steps, drain, 0)

    pltpu.make_async_copy(taken, out_ref, out_sem).wait()

    @pl.when(lender)
    def _():
        for d in range(1, side):
            for k in range(2 * (chips - 1)):
                sent(gathered.at[0, pl.ds(0, width)], s_lend.at[d - 1, k])

    pl.when(jnp.logical_and(owner, zone > 0))(lambda: sent(last, s_last))

    @pl.when(jnp.logical_and(owner, zone > 1))
    def _():
        sent(last, s_chain.at[2])
        for d in range(1, side):
            sent(last, s_hint.at[d - 1])

    @pl.when(jnp.logical_and(jnp.logical_not(owner), zone > 1))
    def _():
        sent(last, s_chain.at[0])
        for z in range(steps - 3):
            pl.when(helps_back(z))(lambda: sent(last, s_help.at[z]))


def body(rhs, factors, diag_inv):
    n_row, n_col = lax.axis_size("row"), lax.axis_size("col")
    rows_dev, width = rhs.shape
    cols = factors.shape[1]
    steps, block = diag_inv.shape[:2]
    pieces, chips, side = block // cols, n_row // 2, n_col // steps
    step_rows = rows_dev // CHUNKS
    dma = pltpu.SemaphoreType.DMA
    taken = pl.pallas_call(
        functools.partial(kernel, n_row, n_col, steps, block),
        out_shape=jax.ShapeDtypeStruct(rhs.shape, F32),
        in_specs=[pl.BlockSpec(memory_space=pl.ANY)] * 3,
        out_specs=pl.BlockSpec(memory_space=pl.ANY),
        scratch_shapes=[
            pltpu.VMEM(rhs.shape, F32),
            pltpu.VMEM(factors.shape, BF16),
            pltpu.VMEM((GATHER, 2, chips, step_rows, cols), BF16),
            pltpu.VMEM(rhs.shape, F32),
            pltpu.VMEM((block, block), F32),
            pltpu.VMEM((block, block), BF16),
            pltpu.VMEM((block, block), BF16),
            pltpu.VMEM((block, block), BF16),
            pltpu.VMEM((block, block), BF16),
            pltpu.VMEM((n_row, block, cols), BF16),
            pltpu.VMEM((steps, width, block), BF16),
            pltpu.VMEM((width, block), BF16),
            pltpu.VMEM((block, width), F32),
            pltpu.VMEM((width, block), F32),
            pltpu.VMEM((2, chips * width, cols), BF16),
            pltpu.VMEM((CHUNKS, step_rows, chips * width), BF16),
            pltpu.VMEM((CHUNKS, step_rows, chips * width), BF16),
            pltpu.VMEM((CHUNKS, step_rows, chips * width), F32),
            pltpu.VMEM((CHUNKS, chips - 1, step_rows, width), BF16),
            pltpu.VMEM((CHUNKS, chips - 1, step_rows, width), BF16),
            dma, dma, dma((2, chips - 1)), dma((n_row, CUTS + 1)), dma((n_row,)),
            dma((3,)), dma((steps, side - 1)), dma((steps, pieces)), dma((side - 1, 2 * (chips - 1))),
            dma((steps,)), dma((side - 1,)), dma((steps, SUBS)), dma((SUBS,)), dma,
            dma((SUBS,)), dma((n_row, SUBS)),
            dma((2,)), dma((CHUNKS,)), dma((CHUNKS, chips - 1)), dma((CHUNKS, chips - 1)),
            dma((GATHER, chips)), dma((GATHER, chips)), dma((GATHER, chips - 1)), dma((4,)), dma,
        ],
        compiler_params=pltpu.CompilerParams(
            collective_id=0, has_side_effects=True, vmem_limit_bytes=50 * 1024 * 1024
        ),
    )(rhs, factors, diag_inv)
    return taken


def solution(mesh):
    placed = (P("col", "row"), P("col", "row"), P())
    return jax.shard_map(
        body, mesh=mesh, in_specs=placed, out_specs=P("col", "row"), check_vma=False
    )
```
